32 devices in a mesh: batch: 4 (over x, core), seq: 8 (over z, y).
Axes of the slice: x: 2, y: 2, z: 4, core: 2. Of those that a mesh axis runs over, the one named last changes fastest.
Arguments:
- sequences: bfloat16 [4, 2048, 256], P('batch', 'seq'), may hold values from -6 to 6
- filter_taps: float32 [2048, 256], P('seq'), may hold values from -0.125 to 0.125
- w_in: bfloat16 [256, 768], replicated, may hold values from -0.375 to 0.375
- w_out: bfloat16 [256, 256], replicated, may hold values from -0.375 to 0.375
- grad_out: bfloat16 [4, 2048, 256], P('batch', 'seq'), may hold values from -6 to 6
Outputs:
- layer_out: bfloat16 [4, 2048, 256], P('batch', 'seq')
- filter_grad: float32 [2, 16, 256, 256], P(None, 'seq', 'batch')
The draws below stay inside these ranges and needn't reach their ends.
All inputs are finite; a program needn't handle non-finite values.
Results may differ from the reference program's by a relative error of at most 0.0049.
Values sent between devices are 32-bit elements; how exact they have to be, the bound alone decides.
A program may use at most 64 MiB of HBM per device.

```python
import jax
import jax.numpy as jnp
from jax import lax

D = 256
SEQS = 4
LENGTH = 2048
N_SEQ = 8


def block_levels(stream_key, extent, split, least, high):
    gain = 1.0
    for position, parts in split:
        steps = jax.random.uniform(jax.random.fold_in(jax.random.fold_in(stream_key, 6), position), (parts,), jnp.float32, least / len(split), high / len(split))
        gain = gain * jnp.repeat(jnp.exp(steps), extent[position] // parts).reshape((-1,) + (1,) * (len(extent) - 1 - position))
    return gain


def noise(own_key, dims, deviation, bound, cuts=(), held_as=jnp.bfloat16):
    array = deviation * jax.random.normal(own_key, dims, jnp.float32)
    if cuts:
        array = array * block_levels(own_key, dims, cuts, -0.22, 0.18)
    return jnp.clip(array, -bound, bound).astype(held_as)


def setup_inputs(seed: int = 0) -> dict:
    arg_keys = jax.random.split(jax.random.key(seed), 6)
    sequences = noise(arg_keys[0], (SEQS, LENGTH, D), 1.0, 6.0, ((0, 4), (1, 8)))
    filter_taps = noise(arg_keys[1], (LENGTH, D), LENGTH ** -0.5, 0.125, ((0, 8),), jnp.float32)
    w_in = noise(arg_keys[2], (D, 3 * D), D ** -0.5, 0.375)
    w_out = noise(arg_keys[3], (D, D), D ** -0.5, 0.375)
    grad_out = noise(arg_keys[4], (SEQS, LENGTH, D), 1.0, 6.0, ((0, 4), (1, 8)))
    return {"sequences": sequences, "filter_taps": filter_taps, "w_in": w_in, "w_out": w_out, "grad_out": grad_out}


def spectrum_of(signal):
    padded = jnp.concatenate([signal, jnp.zeros_like(signal)], axis=0)
    return jnp.fft.fft(padded, axis=0)


def reference(sequences, filter_taps, w_in, w_out, grad_out):
    channels = w_out.shape[0]
    length = sequences.shape[1]
    full_span = 2 * length
    taps_spec = spectrum_of(filter_taps)

    def one_sequence(totals, inputs):
        tokens, cotangent = inputs
        projected = jnp.dot(tokens, w_in, preferred_element_type=jnp.float32)
        queries = projected[:, :channels]
        signal = projected[:, channels:2 * channels] * projected[:, 2 * channels:]
        signal_spec = spectrum_of(signal)
        convolved = jnp.real(jnp.fft.ifft(taps_spec * signal_spec, axis=0))[:length]
        gated = (queries * convolved).astype(jnp.bfloat16)
        layer_out = jnp.dot(gated, w_out, preferred_element_type=jnp.float32).astype(jnp.bfloat16)
        back_grad = jnp.dot(cotangent, w_out.T, preferred_element_type=jnp.float32)
        conv_grad = queries * back_grad
        grad_spec = spectrum_of(conv_grad)
        product = jnp.conj(signal_spec) * grad_spec
        return (totals[0] + jnp.real(product), totals[1] + jnp.imag(product)), layer_out

    empty_sum = jnp.zeros((full_span, channels), jnp.float32)
    (real_sum, imag_sum), layer_out = lax.scan(one_sequence, (empty_sum, empty_sum), (sequences, grad_out))
    freq_rows = 2 * N_SEQ

    def arrange(summed):
        return summed.reshape(full_span // freq_rows, freq_rows, channels).transpose(1, 0, 2) / full_span

    filter_grad = jnp.stack([arrange(real_sum), arrange(imag_sum)], axis=0)
    return layer_out, filter_grad
```

```python
import functools
import math

import jax
import jax.numpy as jnp
import numpy as np
from jax import lax
from jax.experimental import pallas as pl
from jax.experimental.pallas import tpu as pltpu
from jax.sharding import PartitionSpec as P

precise = lax.Precision.HIGHEST


def counting(length):
    return jnp.arange(length, dtype=jnp.int32)


def phase_table(left_index, right_index, period):
    product = left_index[:, None] * right_index[None, :] % period
    angles = product.astype(jnp.float32) * (2.0 * math.pi / period)
    return (jnp.cos(angles), jnp.sin(angles))


def split_length(length):
    outer_len = math.isqrt(length)
    while length % outer_len:
        outer_len -= 1
    return (outer_len, length // outer_len)


def local_forward(spectrum):
    groups = spectrum.shape[0]
    length = spectrum.shape[1]
    channels = spectrum.shape[3]
    outer_len, inner_len = split_length(length)
    shaped = spectrum.reshape(groups, outer_len, inner_len, 2, channels)
    real_in = shaped[:, :, :, 0]
    imag_in = shaped[:, :, :, 1]
    cos_outer, sin_outer = phase_table(counting(outer_len), counting(outer_len), outer_len)
    real_mid = jnp.einsum("jm,fmnc->fjnc", cos_outer, real_in, precision=precise) + jnp.einsum(
        "jm,fmnc->fjnc", sin_outer, imag_in, precision=precise
    )
    imag_mid = jnp.einsum("jm,fmnc->fjnc", cos_outer, imag_in, precision=precise) - jnp.einsum(
        "jm,fmnc->fjnc", sin_outer, real_in, precision=precise
    )
    cos_twist, sin_twist = phase_table(counting(outer_len), counting(inner_len), length)
    cos_twist = cos_twist[None, :, :, None]
    sin_twist = sin_twist[None, :, :, None]
    real_turned = real_mid * cos_twist + imag_mid * sin_twist
    imag_turned = imag_mid * cos_twist - real_mid * sin_twist
    cos_inner, sin_inner = phase_table(counting(inner_len), counting(inner_len), inner_len)
    real_out = jnp.einsum("kn,fjnc->fkjc", cos_inner, real_turned, precision=precise) + jnp.einsum(
        "kn,fjnc->fkjc", sin_inner, imag_turned, precision=precise
    )
    imag_out = jnp.einsum("kn,fjnc->fkjc", cos_inner, imag_turned, precision=precise) - jnp.einsum(
        "kn,fjnc->fkjc", sin_inner, real_turned, precision=precise
    )
    return jnp.stack([real_out, imag_out], axis=3).reshape(groups, length, 2, channels)


def local_inverse(real_spec, imag_spec):
    groups = real_spec.shape[0]
    length = real_spec.shape[1]
    channels = real_spec.shape[2]
    outer_len, inner_len = split_length(length)
    real_grid = real_spec.reshape(groups, inner_len, outer_len, channels)
    imag_grid = imag_spec.reshape(groups, inner_len, outer_len, channels)
    cos_inner, sin_inner = phase_table(counting(inner_len), counting(inner_len), inner_len)
    real_mid = jnp.einsum("nk,fkjc->fjnc", cos_inner, real_grid, precision=precise) - jnp.einsum(
        "nk,fkjc->fjnc", sin_inner, imag_grid, precision=precise
    )
    imag_mid = jnp.einsum("nk,fkjc->fjnc", cos_inner, imag_grid, precision=precise) + jnp.einsum(
        "nk,fkjc->fjnc", sin_inner, real_grid, precision=precise
    )
    cos_twist, sin_twist = phase_table(counting(outer_len), counting(inner_len), length)
    cos_twist = cos_twist[None, :, :, None]
    sin_twist = sin_twist[None, :, :, None]
    real_turned = real_mid * cos_twist - imag_mid * sin_twist
    imag_turned = imag_mid * cos_twist + real_mid * sin_twist
    cos_outer, sin_outer = phase_table(counting(outer_len), counting(outer_len), outer_len)
    real_out = jnp.einsum("mj,fjnc->fmnc", cos_outer, real_turned, precision=precise) - jnp.einsum(
        "mj,fjnc->fmnc", sin_outer, imag_turned, precision=precise
    )
    imag_out = jnp.einsum("mj,fjnc->fmnc", cos_outer, imag_turned, precision=precise) + jnp.einsum(
        "mj,fjnc->fmnc", sin_outer, real_turned, precision=precise
    )
    return (real_out.reshape(groups, length, channels), imag_out.reshape(groups, length, channels))


def forward_spectrum(columns, residue_order):
    shards = lax.axis_size("seq")
    local_len = columns.shape[0]
    block_rows = local_len // shards
    freq_rows = 2 * shards
    full_span = freq_rows * local_len
    glob_rows = lax.axis_index("seq") * block_rows + counting(block_rows)
    pieces = lax.all_to_all(columns[None], "seq", split_axis=1, concat_axis=0, tiled=True)
    cos_first, sin_first = phase_table(residue_order, counting(shards), freq_rows)
    real_part = jnp.einsum("ka,amc->kmc", cos_first, pieces[:, :, 0], precision=precise)
    imag_part = -jnp.einsum("ka,amc->kmc", sin_first, pieces[:, :, 0], precision=precise)
    cos_twist, sin_twist = phase_table(residue_order, glob_rows, full_span)
    cos_twist = cos_twist[:, :, None]
    sin_twist = sin_twist[:, :, None]
    real_turned = real_part * cos_twist + imag_part * sin_twist
    imag_turned = imag_part * cos_twist - real_part * sin_twist
    packed = jnp.stack([real_turned, imag_turned], axis=2)
    return local_forward(lax.all_to_all(packed, "seq", split_axis=0, concat_axis=1, tiled=True))


def inverse_signal(real_spec, imag_spec, residue_order):
    shards = lax.axis_size("seq")
    pair_rows = real_spec.shape[0]
    local_len = real_spec.shape[1]
    freq_rows = pair_rows * shards
    full_span = freq_rows * local_len
    real_part, imag_part = local_inverse(real_spec, imag_spec)
    pair_index = lax.dynamic_slice_in_dim(
        residue_order, lax.axis_index("seq") * pair_rows, pair_rows
    )
    cos_twist, sin_twist = phase_table(pair_index, counting(local_len), full_span)
    cos_twist = cos_twist[:, :, None]
    sin_twist = sin_twist[:, :, None]
    real_turned = real_part * cos_twist - imag_part * sin_twist
    imag_turned = imag_part * cos_twist + real_part * sin_twist
    packed = jnp.stack([real_turned, imag_turned], axis=2)
    pieces = lax.all_to_all(packed, "seq", split_axis=1, concat_axis=0, tiled=True)
    cos_last, sin_last = phase_table(counting(shards), residue_order, freq_rows)
    summed = jnp.einsum("ak,kmc->amc", cos_last, pieces[:, :, 0], precision=precise) - jnp.einsum(
        "ak,kmc->amc", sin_last, pieces[:, :, 1], precision=precise
    )
    columns = summed * (1.0 / full_span)
    placed = lax.all_to_all(columns, "seq", split_axis=0, concat_axis=1, tiled=True)
    return placed[0]


def local(sequences, filter_taps, w_in, w_out, grad_out):
    channels = w_out.shape[0]
    groups = lax.axis_size("batch")
    shards = lax.axis_size("seq")
    projected = jnp.dot(sequences[0], w_in, preferred_element_type=jnp.float32)
    queries = projected[:, :channels]
    signal = projected[:, channels : 2 * channels] * projected[:, 2 * channels :]
    back_grad = lax.dot_general(
        grad_out[0], w_out, (((1,), (1,)), ((), ())), preferred_element_type=jnp.float32
    )
    conv_grad = queries * back_grad
    order_table = np.arange(2 * shards)
    residue_order = jnp.asarray(order_table, jnp.int32)
    part_width = channels // groups
    filter_part = lax.dynamic_slice_in_dim(
        filter_taps, lax.axis_index("batch") * part_width, part_width, 1
    )
    signal_spec = forward_spectrum(signal[:, None], residue_order)
    grad_spec = forward_spectrum(conv_grad[:, None], residue_order)
    taps_spec = forward_spectrum(filter_part[:, None], residue_order)
    taps_spec = lax.all_gather(taps_spec, "batch", axis=3, tiled=True)
    real_sig = signal_spec[:, :, 0]
    imag_sig = signal_spec[:, :, 1]
    real_taps = taps_spec[:, :, 0]
    imag_taps = taps_spec[:, :, 1]
    real_conv = real_taps * real_sig - imag_taps * imag_sig
    imag_conv = real_taps * imag_sig + imag_taps * real_sig
    convolved = inverse_signal(real_conv, imag_conv, residue_order)
    gated = (queries * convolved).astype(jnp.bfloat16)
    layer_out = jnp.dot(gated, w_out, preferred_element_type=jnp.float32).astype(jnp.bfloat16)
    factor = 1.0 / (signal_spec.shape[0] * shards * signal_spec.shape[1])
    real_grad = grad_spec[:, :, 0]
    imag_grad = grad_spec[:, :, 1]
    grad_terms = jnp.stack(
        [
            (real_sig * real_grad + imag_sig * imag_grad) * factor,
            (real_sig * imag_grad - imag_sig * real_grad) * factor,
        ],
        axis=0,
    )
    filter_grad = lax.psum_scatter(grad_terms, "batch", scatter_dimension=2, tiled=True)
    return (layer_out[None], filter_grad)


MESH = pl.DeviceIdType.MESH
FULL_TILE = 8


def wide_tables(block_rows, freq_rows):
    residues = freq_rows // 2 + 1
    span = block_rows * freq_rows
    near = np.arange(block_rows)
    angles = 2.0 * np.pi * (np.outer(near, near) % block_rows) / block_rows
    cos_part, sin_part = np.cos(angles), np.sin(angles)
    matrix = np.block([[cos_part, -sin_part], [sin_part, cos_part]])
    high = matrix.astype(jnp.bfloat16)
    low = (matrix - high.astype(np.float64)).astype(jnp.bfloat16)
    twist_angles = 2.0 * np.pi * np.outer(np.arange(residues), near) / span
    twist = np.stack([np.cos(twist_angles), np.sin(twist_angles)], axis=0).astype(np.float32)
    twist = np.ascontiguousarray(
        np.broadcast_to(twist[:, :, None, :], (2, residues, FULL_TILE, block_rows))
    )
    return (high, low, twist)


def grouped_sum(items, weights):
    groups = {}
    for item, weight in zip(items, weights):
        size = round(abs(weight), 12)
        if size == 0.0:
            continue
        positive, total = groups.get(size, (None, None))
        if total is None:
            groups[size] = (weight > 0, item)
        elif positive == (weight > 0):
            groups[size] = (positive, total + item)
        else:
            groups[size] = (positive, total - item)
    result = None
    for size in sorted(groups, reverse=True):
        positive, total = groups[size]
        term = total if size == 1.0 else total * size
        if result is None:
            result = term if positive else -term
        else:
            result = result + term if positive else result - term
    return result


def kernel(
    groups, shards, part,
    x_hbm, taps_hbm, w_in_hbm, w_out_hbm, cot_hbm, high_hbm, low_hbm, twist_hbm,
    out_hbm, spec_out,
    x_ref, taps_ref, w_in_ref, w_out_ref, cot_ref, high_ref, low_ref, twist_ref, out_ref,
    load_sems, store_sems, query_buf, sig_send, cot_send, tap_send, sig_buf, cot_buf, tap_buf,
    conv_send, conv_buf, spec_send, near_sig, near_tap, near_conv,
    work, sig_spec, tap_spec, send_sems, recv_sems, late,
):
    count = groups * shards
    rows = x_ref.shape[1]
    channels = w_out_ref.shape[0]
    half = shards // 2
    quarter = shards // 4
    lanes = rows // groups
    my_group = lax.axis_index("batch")
    my_shard = lax.axis_index("seq")
    me = my_group * shards + my_shard
    my_half = lax.div(my_shard, half)
    lower = my_half == 0
    upper = my_half == 1
    is_last = my_shard >= shards - quarter
    near_me = my_group * half + lax.rem(my_shard, half)
    barrier = pltpu.get_barrier_semaphore()

    def across(step):
        turn = step // groups
        shard = (1 - my_half) * half + turn // quarter * quarter + lax.rem(my_shard + turn, quarter)
        return (lax.rem(my_group + step, groups), shard)

    def level(step):
        turn = step // groups
        shard = lax.div(my_shard, quarter) * quarter + lax.rem(my_shard + turn, quarter)
        return (lax.rem(my_group + step, groups), shard)

    def beside(step):
        turn = step // groups
        plane = 2 * my_half + 1 - lax.rem(lax.div(my_shard, quarter), 2)
        return (lax.rem(my_group + step, groups), plane * quarter + lax.rem(my_shard + turn, quarter))

    wide = groups * quarter
    far_first = [across(step) for step in range(wide)]
    far_second = [across(step) for step in range(wide, 2 * wide)]
    far = far_first + far_second
    same_plane = [level(step) for step in range(1, wide)]
    next_plane = [beside(step) for step in range(wide)]
    near = next_plane + same_plane

    def signal(semaphore, peers):
        for group, shard in peers:
            pl.semaphore_signal(semaphore, inc=1, device_id=(group, shard), device_id_type=MESH)

    @pl.when(jnp.logical_not(is_last))
    def _():
        signal(barrier, far + near)

    @pl.when(is_last)
    def _():
        signal(barrier, same_plane)

    loads = [
        pltpu.make_async_copy(source, target, load_sems.at[n])
        for n, (source, target) in enumerate(
            (
                (x_hbm, x_ref),
                (w_in_hbm, w_in_ref),
                (taps_hbm, taps_ref),
                (w_out_hbm, w_out_ref),
                (cot_hbm, cot_ref),
                (twist_hbm, twist_ref),
                (high_hbm, high_ref),
                (low_hbm, low_ref),
            )
        )
    ]
    for load in loads:
        load.start()

    def push(source, target, slot, peers):
        for group, shard in peers:
            pltpu.make_async_remote_copy(
                src_ref=source.at[group * shards + shard],
                dst_ref=target.at[me],
                send_sem=send_sems.at[slot],
                recv_sem=recv_sems.at[slot],
                device_id=(group, shard),
                device_id_type=MESH,
            ).start()

    def push_taps(offsets):
        for offset in offsets:
            shard = lax.rem(my_shard + offset, shards)
            pltpu.make_async_remote_copy(
                src_ref=tap_send.at[my_group * shards + shard],
                dst_ref=tap_buf.at[my_shard],
                send_sem=send_sems.at[1],
                recv_sem=recv_sems.at[1],
                device_id=(my_group, shard),
                device_id_type=MESH,
            ).start()

    def bundle(source, target, slot, many):
        return pltpu.make_async_remote_copy(
            src_ref=source.at[pl.ds(0, many)],
            dst_ref=target.at[pl.ds(0, many)],
            send_sem=send_sems.at[slot],
            recv_sem=recv_sems.at[slot],
            device_id=(my_group, my_shard),
            device_id_type=MESH,
        )

    loads[0].wait()
    loads[1].wait()
    projected = lax.dot_general(
        w_in_ref[...], x_ref[0], (((0,), (1,)), ((), ())), preferred_element_type=jnp.float32
    )
    queries = projected[:channels]
    query_buf[...] = queries
    signal_part = projected[channels : 2 * channels] * projected[2 * channels :]
    sig_send[...] = signal_part.reshape(count, part, rows)
    loads[2].wait()
    tap_send[...] = taps_ref[...].T.reshape(count, part, rows)
    pl.semaphore_wait(barrier, jnp.where(is_last, count - 1, count - 1 - wide))

    @pl.when(is_last)
    def _():
        signal(late, far + next_plane)

    @pl.when(lower)
    def _():
        push(sig_send, sig_buf, 0, far_first + near)
        for group, shard in near:
            pltpu.make_async_remote_copy(
                src_ref=sig_send.at[group * shards + shard + half],
                dst_ref=near_sig.at[near_me],
                send_sem=send_sems.at[5],
                recv_sem=recv_sems.at[5],
                device_id=(group, shard),
                device_id_type=MESH,
            ).start()
        near_sig[near_me] = sig_send[me + half]
        for offset in range(1, half):
            shard = lax.rem(my_shard + offset, half)
            pltpu.make_async_remote_copy(
                src_ref=tap_send.at[my_group * shards + shard + half],
                dst_ref=near_tap.at[my_shard],
                send_sem=send_sems.at[6],
                recv_sem=recv_sems.at[6],
                device_id=(my_group, shard),
                device_id_type=MESH,
            ).start()
        near_tap[my_shard] = tap_send[me + half]

    @pl.when(upper)
    def _():
        push(sig_send, sig_buf, 0, far + same_plane)

    sig_buf[me] = sig_send[me]
    tap_buf[my_shard] = tap_send[me]
    loads[3].wait()
    loads[4].wait()
    back = lax.dot_general(
        w_out_ref[...], cot_ref[0], (((1,), (1,)), ((), ())), preferred_element_type=jnp.float32
    )
    cot_send[...] = (queries * back).reshape(count, part, rows)

    @pl.when(jnp.logical_not(is_last))
    def _():
        pl.semaphore_wait(late, wide)

    @pl.when(lower)
    def _():
        push(sig_send, sig_buf, 0, far_second)

    @pl.when(upper)
    def _():
        push(sig_send, sig_buf, 0, next_plane)

    push(cot_send, cot_buf, 2, far)
    push_taps(range(1, shards))
    push(cot_send, cot_buf, 2, near)
    cot_buf[me] = cot_send[me]

    def multiply(value):
        top = value.astype(jnp.bfloat16)
        rest = (value - top.astype(jnp.float32)).astype(jnp.bfloat16)
        high = high_ref[...]
        return (
            jnp.dot(top, high, preferred_element_type=jnp.float32)
            + jnp.dot(rest, high, preferred_element_type=jnp.float32)
            + jnp.dot(top, low_ref[...], preferred_element_type=jnp.float32)
        )

    for load in loads[5:]:
        load.wait()

    def forward(blocks, height):
        bands = len(blocks)
        turns = math.pi / bands
        for index in range(bands + 1):
            real_part = grouped_sum(
                blocks, [math.cos(turns * (a * index % (2 * bands))) for a in range(bands)]
            )
            imag_part = grouped_sum(
                blocks, [-math.sin(turns * (a * index % (2 * bands))) for a in range(bands)]
            )
            cos_t = twist_ref[0, index * (shards // bands)][None]
            sin_t = twist_ref[1, index * (shards // bands)][None]
            if imag_part is None:
                real_turned = real_part * cos_t
                imag_turned = -(real_part * sin_t)
            else:
                real_turned = real_part * cos_t + imag_part * sin_t
                imag_turned = imag_part * cos_t - real_part * sin_t
            place_at = pl.ds(index * height, height)
            work[place_at, :rows] = real_turned.reshape(height, rows)
            work[place_at, rows:] = imag_turned.reshape(height, rows)
        return multiply(work[pl.ds(0, (bands + 1) * height), :])

    height = groups * part

    def convolve(bands, target, stride):
        turns = math.pi / bands
        scale = 1.0 / (2 * bands * rows)
        used = pl.ds(0, (bands + 1) * height)
        for index in range(bands + 1):
            weight = scale if index in (0, bands) else 2.0 * scale
            tap_part = tap_spec[pl.ds(index * part, part), :] * weight
            real_tap = tap_part[None, :, :rows]
            imag_tap = tap_part[None, :, rows:]
            sig_part = sig_spec[pl.ds(index * height, height), :].reshape(groups, part, 2 * rows)
            real_sig = sig_part[:, :, :rows]
            imag_sig = sig_part[:, :, rows:]
            place_at = pl.ds(index * height, height)
            work[place_at, :rows] = (real_tap * real_sig - imag_tap * imag_sig).reshape(height, rows)
            work[place_at, rows:] = -(real_tap * imag_sig + imag_tap * real_sig).reshape(height, rows)
        work[used, :] = multiply(work[used, :])
        real_items = []
        imag_items = []
        for index in range(bands + 1):
            piece = work[pl.ds(index * height, height), :].reshape(groups, part, 2 * rows)
            cos_t = twist_ref[0, index * (shards // bands)][None]
            sin_t = twist_ref[1, index * (shards // bands)][None]
            real_items.append(piece[:, :, :rows] * cos_t + piece[:, :, rows:] * sin_t)
            imag_items.append(piece[:, :, :rows] * sin_t - piece[:, :, rows:] * cos_t)
        for a in range(bands):
            value = grouped_sum(
                real_items + imag_items,
                [math.cos(turns * (a * i % (2 * bands))) for i in range(bands + 1)]
                + [-math.sin(turns * (a * i % (2 * bands))) for i in range(bands + 1)],
            )
            for group in range(groups):
                target[group * stride + a] = value[group]

    @pl.when(lower)
    def _():
        bundle(sig_send, near_sig, 5, groups * half - 1).wait_recv()
        by_source = near_sig[...].reshape(groups, half, part, rows)
        sig_spec[pl.ds(0, (half + 1) * height), :] = forward(
            [by_source[:, a] for a in range(half)], height
        )
        bundle(tap_send, near_tap, 6, half - 1).wait_recv()
        tap_blocks = near_tap[...]
        tap_spec[pl.ds(0, (half + 1) * part), :] = forward(
            [tap_blocks[a][None] for a in range(half)], part
        )
        convolve(half, near_conv, half)
        for group, shard in near:
            pltpu.make_async_remote_copy(
                src_ref=near_conv.at[group * half + shard],
                dst_ref=conv_buf.at[me + half],
                send_sem=send_sems.at[7],
                recv_sem=recv_sems.at[3],
                device_id=(group, shard),
                device_id_type=MESH,
            ).start()
        conv_buf[me + half] = near_conv[near_me]

    bundle(sig_send, sig_buf, 0, count - 1).wait_recv()
    by_source = sig_buf[...].reshape(groups, shards, part, rows)
    sig_spec[...] = forward([by_source[:, a] for a in range(shards)], height)

    bundle(tap_send, tap_buf, 1, shards - 1).wait_recv()
    tap_blocks = tap_buf[...]
    tap_spec[...] = forward([tap_blocks[a][None] for a in range(shards)], part)
    convolve(shards, conv_send, shards)

    @pl.when(lower)
    def _():
        push(conv_send, conv_buf, 3, far)

    push(conv_send, conv_buf, 3, near)
    conv_buf[me] = conv_send[me]

    factor = 1.0 / (2 * shards * rows)
    residues = shards + 1
    bundle(cot_send, cot_buf, 2, count - 1).wait_recv()
    by_source = cot_buf[...].reshape(groups, shards, part, rows)
    work[...] = forward([by_source[:, a] for a in range(shards)], height)
    real_spec = []
    imag_spec = []
    for index in range(residues):
        place_at = pl.ds(index * height, height)
        sig_part = (sig_spec[place_at, :] * factor).reshape(groups, part, 2 * rows)
        cot_part = work[place_at, :].reshape(groups, part, 2 * rows)
        real_sig, imag_sig = sig_part[:, :, :rows], sig_part[:, :, rows:]
        real_cot, imag_cot = cot_part[:, :, :rows], cot_part[:, :, rows:]
        real_spec.append(jnp.sum(real_sig * real_cot + imag_sig * imag_cot, axis=0))
        imag_spec.append(jnp.sum(real_sig * imag_cot - imag_sig * real_cot, axis=0))
    row = lax.broadcasted_iota(jnp.int32, (rows, rows), 0)
    column = lax.broadcasted_iota(jnp.int32, (rows, rows), 1)
    reverse = jnp.where(row + column == rows - 1, 1.0, 0.0).astype(jnp.bfloat16)
    straight = jnp.concatenate(
        real_spec[1:shards] + [-piece for piece in imag_spec[1:shards]], axis=0
    )
    turned = None
    for _ in range(3):
        top = straight.astype(jnp.bfloat16)
        straight = straight - top.astype(jnp.float32)
        term = jnp.dot(top, reverse, preferred_element_type=jnp.float32)
        turned = term if turned is None else turned + term
    for index in range(shards - 1, 0, -1):
        low_row = (index - 1) * part
        real_spec.append(turned[low_row : low_row + part])
        low_row += (shards - 1) * part
        imag_spec.append(turned[low_row : low_row + part])
    for shard in range(shards):
        for group in range(groups):
            pieces = [
                spec[index][:, group * lanes : (group + 1) * lanes]
                for spec in (real_spec, imag_spec)
                for index in (2 * shard, 2 * shard + 1)
            ]
            spec_send[group * shards + shard] = jnp.concatenate(pieces, axis=1)
    push(spec_send, spec_out, 4, far + near)
    own = pltpu.make_async_copy(spec_send.at[me], spec_out.at[me], store_sems.at[0])
    own.start()

    @pl.when(lower)
    def _():
        bundle(conv_send, conv_buf, 3, count - 2).wait_recv()

    @pl.when(upper)
    def _():
        bundle(conv_send, conv_buf, 3, count - 1).wait_recv()

    gated = (query_buf[...] * conv_buf[...].reshape(channels, rows)).astype(jnp.bfloat16)
    out_ref[0] = lax.dot_general(
        gated, w_out_ref[...], (((0,), (0,)), ((), ())), preferred_element_type=jnp.float32
    ).astype(jnp.bfloat16)

    store = pltpu.make_async_copy(out_ref, out_hbm, store_sems.at[1])
    store.start()
    bundle(sig_send, sig_buf, 0, count - 1).wait_send()
    bundle(tap_send, tap_buf, 1, shards - 1).wait_send()
    bundle(cot_send, cot_buf, 2, count - 1).wait_send()

    @pl.when(lower)
    def _():
        bundle(conv_send, conv_buf, 3, count - 1).wait_send()
        bundle(sig_send, near_sig, 5, groups * half - 1).wait_send()
        bundle(tap_send, near_tap, 6, half - 1).wait_send()
        bundle(near_conv, conv_buf, 7, groups * half - 1).wait_send()

    @pl.when(upper)
    def _():
        bundle(conv_send, conv_buf, 3, groups * half - 1).wait_send()

    bundle(spec_send, spec_out, 4, count - 1).wait_send()
    own.wait()
    store.wait()
    bundle(spec_send, spec_out, 4, count - 1).wait_recv()


def finish(raw_hbm, spec_hbm, out_hbm, grad_hbm, raw_buf, spec_buf, grad_buf, load_sems, store_sems):
    load_spec = pltpu.make_async_copy(spec_hbm, spec_buf, load_sems.at[0])
    load_raw = pltpu.make_async_copy(raw_hbm, raw_buf, load_sems.at[1])
    load_spec.start()
    load_raw.start()
    count, part, width = spec_buf.shape
    stores = []
    load_spec.wait()
    for kind in range(2):
        piece = spec_buf[:, :, kind * (width // 2) : (kind + 1) * (width // 2)]
        grad_buf[kind] = piece.reshape(count * part, width // 2).T.reshape(grad_buf.shape[1:])
        store = pltpu.make_async_copy(grad_buf.at[kind], grad_hbm.at[kind], store_sems.at[kind])
        store.start()
        stores.append(store)
        if kind == 0:
            load_raw.wait()
            store = pltpu.make_async_copy(raw_buf, out_hbm, store_sems.at[2])
            store.start()
            stores.append(store)
    for store in stores:
        store.wait()


def direct(sequences, filter_taps, w_in, w_out, grad_out):
    groups = lax.axis_size("batch")
    shards = lax.axis_size("seq")
    rows = sequences.shape[1]
    channels = w_out.shape[0]
    count = groups * shards
    part = channels // count
    freq_rows = 2 * shards
    residues = shards + 1
    lanes = rows // groups
    high, low, twist = wide_tables(rows, freq_rows)
    operands = (
        sequences, filter_taps, w_in, w_out, grad_out,
        jnp.asarray(high), jnp.asarray(low), jnp.asarray(twist),
    )
    chunk = pltpu.VMEM((count, part, rows), jnp.float32)
    height = groups * part
    anywhere = pl.BlockSpec(memory_space=pl.ANY)
    raw, spectra = pl.pallas_call(
        functools.partial(kernel, groups, shards, part),
        out_shape=(
            jax.ShapeDtypeStruct((1, rows, channels), jnp.bfloat16),
            jax.ShapeDtypeStruct((count, part, rows), jnp.float32),
        ),
        in_specs=[anywhere] * 8,
        out_specs=(anywhere, anywhere),
        scratch_shapes=[
            *(pltpu.VMEM(item.shape, item.dtype) for item in operands),
            pltpu.VMEM((1, rows, channels), jnp.bfloat16),
            pltpu.SemaphoreType.DMA((8,)),
            pltpu.SemaphoreType.DMA((2,)),
            pltpu.VMEM((channels, rows), jnp.float32),
            chunk,
            chunk,
            chunk,
            chunk,
            chunk,
            pltpu.VMEM((shards, part, rows), jnp.float32),
            chunk,
            chunk,
            chunk,
            pltpu.VMEM((count // 2, part, rows), jnp.float32),
            pltpu.VMEM((shards // 2, part, rows), jnp.float32),
            pltpu.VMEM((count // 2, part, rows), jnp.float32),
            pltpu.VMEM((residues * height, 2 * rows), jnp.float32),
            pltpu.VMEM((residues * height, 2 * rows), jnp.float32),
            pltpu.VMEM((residues * part, 2 * rows), jnp.float32),
            pltpu.SemaphoreType.DMA((8,)),
            pltpu.SemaphoreType.DMA((7,)),
            pltpu.SemaphoreType.REGULAR,
        ],
        compiler_params=pltpu.CompilerParams(collective_id=0, has_side_effects=True),
    )(*operands)
    return pl.pallas_call(
        finish,
        out_shape=(
            jax.ShapeDtypeStruct((1, rows, channels), jnp.bfloat16),
            jax.ShapeDtypeStruct((2, 2, lanes, channels), jnp.float32),
        ),
        in_specs=[anywhere] * 2,
        out_specs=(anywhere, anywhere),
        scratch_shapes=[
            pltpu.VMEM(raw.shape, raw.dtype),
            pltpu.VMEM(spectra.shape, spectra.dtype),
            pltpu.VMEM((2, 2, lanes, channels), jnp.float32),
            pltpu.SemaphoreType.DMA((2,)),
            pltpu.SemaphoreType.DMA((3,)),
        ],
    )(raw, spectra)


def body(sequences, filter_taps, w_in, w_out, grad_out):
    groups = lax.axis_size("batch")
    count = groups * lax.axis_size("seq")
    rows = sequences.shape[1]
    fits = (
        sequences.shape[0] == 1
        and w_out.shape[0] == FULL_TILE * count
        and lax.axis_size("seq") % 4 == 0
        and rows % 128 == 0
        and rows % groups == 0
        and 2 * (rows // groups) % 128 == 0
    )
    chosen = direct if fits else local
    return chosen(sequences, filter_taps, w_in, w_out, grad_out)


def solution(mesh):
    placed = (P("batch", "seq", None), P("seq", None), P(), P(), P("batch", "seq", None))
    return jax.shard_map(
        body,
        mesh=mesh,
        in_specs=placed,
        out_specs=(P("batch", "seq", None), P(None, "seq", "batch", None)),
        check_vma=False,
    )
```

```python
import functools
import math

import jax
import jax.numpy as jnp
import numpy as np
from jax import lax
from jax.experimental import pallas as pl
from jax.experimental.pallas import tpu as pltpu
from jax.sharding import PartitionSpec as P

precise = lax.Precision.HIGHEST


def counting(length):
    return jnp.arange(length, dtype=jnp.int32)


def phase_table(left_index, right_index, period):
    product = left_index[:, None] * right_index[None, :] % period
    angles = product.astype(jnp.float32) * (2.0 * math.pi / period)
    return (jnp.cos(angles), jnp.sin(angles))


def split_length(length):
    outer_len = math.isqrt(length)
    while length % outer_len:
        outer_len -= 1
    return (outer_len, length // outer_len)


def local_forward(spectrum):
    groups = spectrum.shape[0]
    length = spectrum.shape[1]
    channels = spectrum.shape[3]
    outer_len, inner_len = split_length(length)
    shaped = spectrum.reshape(groups, outer_len, inner_len, 2, channels)
    real_in = shaped[:, :, :, 0]
    imag_in = shaped[:, :, :, 1]
    cos_outer, sin_outer = phase_table(counting(outer_len), counting(outer_len), outer_len)
    real_mid = jnp.einsum("jm,fmnc->fjnc", cos_outer, real_in, precision=precise) + jnp.einsum(
        "jm,fmnc->fjnc", sin_outer, imag_in, precision=precise
    )
    imag_mid = jnp.einsum("jm,fmnc->fjnc", cos_outer, imag_in, precision=precise) - jnp.einsum(
        "jm,fmnc->fjnc", sin_outer, real_in, precision=precise
    )
    cos_twist, sin_twist = phase_table(counting(outer_len), counting(inner_len), length)
    cos_twist = cos_twist[None, :, :, None]
    sin_twist = sin_twist[None, :, :, None]
    real_turned = real_mid * cos_twist + imag_mid * sin_twist
    imag_turned = imag_mid * cos_twist - real_mid * sin_twist
    cos_inner, sin_inner = phase_table(counting(inner_len), counting(inner_len), inner_len)
    real_out = jnp.einsum("kn,fjnc->fkjc", cos_inner, real_turned, precision=precise) + jnp.einsum(
        "kn,fjnc->fkjc", sin_inner, imag_turned, precision=precise
    )
    imag_out = jnp.einsum("kn,fjnc->fkjc", cos_inner, imag_turned, precision=precise) - jnp.einsum(
        "kn,fjnc->fkjc", sin_inner, real_turned, precision=precise
    )
    return jnp.stack([real_out, imag_out], axis=3).reshape(groups, length, 2, channels)


def local_inverse(real_spec, imag_spec):
    groups = real_spec.shape[0]
    length = real_spec.shape[1]
    channels = real_spec.shape[2]
    outer_len, inner_len = split_length(length)
    real_grid = real_spec.reshape(groups, inner_len, outer_len, channels)
    imag_grid = imag_spec.reshape(groups, inner_len, outer_len, channels)
    cos_inner, sin_inner = phase_table(counting(inner_len), counting(inner_len), inner_len)
    real_mid = jnp.einsum("nk,fkjc->fjnc", cos_inner, real_grid, precision=precise) - jnp.einsum(
        "nk,fkjc->fjnc", sin_inner, imag_grid, precision=precise
    )
    imag_mid = jnp.einsum("nk,fkjc->fjnc", cos_inner, imag_grid, precision=precise) + jnp.einsum(
        "nk,fkjc->fjnc", sin_inner, real_grid, precision=precise
    )
    cos_twist, sin_twist = phase_table(counting(outer_len), counting(inner_len), length)
    cos_twist = cos_twist[None, :, :, None]
    sin_twist = sin_twist[None, :, :, None]
    real_turned = real_mid * cos_twist - imag_mid * sin_twist
    imag_turned = imag_mid * cos_twist + real_mid * sin_twist
    cos_outer, sin_outer = phase_table(counting(outer_len), counting(outer_len), outer_len)
    real_out = jnp.einsum("mj,fjnc->fmnc", cos_outer, real_turned, precision=precise) - jnp.einsum(
        "mj,fjnc->fmnc", sin_outer, imag_turned, precision=precise
    )
    imag_out = jnp.einsum("mj,fjnc->fmnc", cos_outer, imag_turned, precision=precise) + jnp.einsum(
        "mj,fjnc->fmnc", sin_outer, real_turned, precision=precise
    )
    return (real_out.reshape(groups, length, channels), imag_out.reshape(groups, length, channels))


def forward_spectrum(columns, residue_order):
    shards = lax.axis_size("seq")
    local_len = columns.shape[0]
    block_rows = local_len // shards
    freq_rows = 2 * shards
    full_span = freq_rows * local_len
    glob_rows = lax.axis_index("seq") * block_rows + counting(block_rows)
    pieces = lax.all_to_all(columns[None], "seq", split_axis=1, concat_axis=0, tiled=True)
    cos_first, sin_first = phase_table(residue_order, counting(shards), freq_rows)
    real_part = jnp.einsum("ka,amc->kmc", cos_first, pieces[:, :, 0], precision=precise)
    imag_part = -jnp.einsum("ka,amc->kmc", sin_first, pieces[:, :, 0], precision=precise)
    cos_twist, sin_twist = phase_table(residue_order, glob_rows, full_span)
    cos_twist = cos_twist[:, :, None]
    sin_twist = sin_twist[:, :, None]
    real_turned = real_part * cos_twist + imag_part * sin_twist
    imag_turned = imag_part * cos_twist - real_part * sin_twist
    packed = jnp.stack([real_turned, imag_turned], axis=2)
    return local_forward(lax.all_to_all(packed, "seq", split_axis=0, concat_axis=1, tiled=True))


def inverse_signal(real_spec, imag_spec, residue_order):
    shards = lax.axis_size("seq")
    pair_rows = real_spec.shape[0]
    local_len = real_spec.shape[1]
    freq_rows = pair_rows * shards
    full_span = freq_rows * local_len
    real_part, imag_part = local_inverse(real_spec, imag_spec)
    pair_index = lax.dynamic_slice_in_dim(
        residue_order, lax.axis_index("seq") * pair_rows, pair_rows
    )
    cos_twist, sin_twist = phase_table(pair_index, counting(local_len), full_span)
    cos_twist = cos_twist[:, :, None]
    sin_twist = sin_twist[:, :, None]
    real_turned = real_part * cos_twist - imag_part * sin_twist
    imag_turned = imag_part * cos_twist + real_part * sin_twist
    packed = jnp.stack([real_turned, imag_turned], axis=2)
    pieces = lax.all_to_all(packed, "seq", split_axis=1, concat_axis=0, tiled=True)
    cos_last, sin_last = phase_table(counting(shards), residue_order, freq_rows)
    summed = jnp.einsum("ak,kmc->amc", cos_last, pieces[:, :, 0], precision=precise) - jnp.einsum(
        "ak,kmc->amc", sin_last, pieces[:, :, 1], precision=precise
    )
    columns = summed * (1.0 / full_span)
    placed = lax.all_to_all(columns, "seq", split_axis=0, concat_axis=1, tiled=True)
    return placed[0]


def local(sequences, filter_taps, w_in, w_out, grad_out):
    channels = w_out.shape[0]
    groups = lax.axis_size("batch")
    shards = lax.axis_size("seq")
    projected = jnp.dot(sequences[0], w_in, preferred_element_type=jnp.float32)
    queries = projected[:, :channels]
    signal = projected[:, channels : 2 * channels] * projected[:, 2 * channels :]
    back_grad = lax.dot_general(
        grad_out[0], w_out, (((1,), (1,)), ((), ())), preferred_element_type=jnp.float32
    )
    conv_grad = queries * back_grad
    order_table = np.arange(2 * shards)
    residue_order = jnp.asarray(order_table, jnp.int32)
    part_width = channels // groups
    filter_part = lax.dynamic_slice_in_dim(
        filter_taps, lax.axis_index("batch") * part_width, part_width, 1
    )
    signal_spec = forward_spectrum(signal[:, None], residue_order)
    grad_spec = forward_spectrum(conv_grad[:, None], residue_order)
    taps_spec = forward_spectrum(filter_part[:, None], residue_order)
    taps_spec = lax.all_gather(taps_spec, "batch", axis=3, tiled=True)
    real_sig = signal_spec[:, :, 0]
    imag_sig = signal_spec[:, :, 1]
    real_taps = taps_spec[:, :, 0]
    imag_taps = taps_spec[:, :, 1]
    real_conv = real_taps * real_sig - imag_taps * imag_sig
    imag_conv = real_taps * imag_sig + imag_taps * real_sig
    convolved = inverse_signal(real_conv, imag_conv, residue_order)
    gated = (queries * convolved).astype(jnp.bfloat16)
    layer_out = jnp.dot(gated, w_out, preferred_element_type=jnp.float32).astype(jnp.bfloat16)
    factor = 1.0 / (signal_spec.shape[0] * shards * signal_spec.shape[1])
    real_grad = grad_spec[:, :, 0]
    imag_grad = grad_spec[:, :, 1]
    grad_terms = jnp.stack(
        [
            (real_sig * real_grad + imag_sig * imag_grad) * factor,
            (real_sig * imag_grad - imag_sig * real_grad) * factor,
        ],
        axis=0,
    )
    filter_grad = lax.psum_scatter(grad_terms, "batch", scatter_dimension=2, tiled=True)
    return (layer_out[None], filter_grad)


MESH = pl.DeviceIdType.MESH
FULL_TILE = 8


def wide_tables(block_rows, freq_rows):
    residues = freq_rows // 2 + 1
    span = block_rows * freq_rows
    near = np.arange(block_rows)
    angles = 2.0 * np.pi * (np.outer(near, near) % block_rows) / block_rows
    cos_part, sin_part = np.cos(angles), np.sin(angles)
    matrix = np.block([[cos_part, -sin_part], [sin_part, cos_part]])
    high = matrix.astype(jnp.bfloat16)
    low = (matrix - high.astype(np.float64)).astype(jnp.bfloat16)
    twist_angles = 2.0 * np.pi * np.outer(np.arange(residues), near) / span
    twist = np.stack([np.cos(twist_angles), np.sin(twist_angles)], axis=0).astype(np.float32)
    twist = np.ascontiguousarray(
        np.broadcast_to(twist[:, :, None, :], (2, residues, FULL_TILE, block_rows))
    )
    return (high, low, twist)


def grouped_sum(items, weights):
    groups = {}
    for item, weight in zip(items, weights):
        size = round(abs(weight), 12)
        if size == 0.0:
            continue
        positive, total = groups.get(size, (None, None))
        if total is None:
            groups[size] = (weight > 0, item)
        elif positive == (weight > 0):
            groups[size] = (positive, total + item)
        else:
            groups[size] = (positive, total - item)
    result = None
    for size in sorted(groups, reverse=True):
        positive, total = groups[size]
        term = total if size == 1.0 else total * size
        if result is None:
            result = term if positive else -term
        else:
            result = result + term if positive else result - term
    return result


def kernel(
    groups, shards, part,
    x_hbm, taps_hbm, w_in_hbm, w_out_hbm, cot_hbm, high_hbm, low_hbm, twist_hbm,
    out_hbm, spec_out,
    x_ref, taps_ref, w_in_ref, w_out_ref, cot_ref, high_ref, low_ref, twist_ref, out_ref,
    load_sems, store_sems, query_buf, sig_send, cot_send, tap_send, sig_buf, cot_buf, tap_buf,
    conv_send, conv_buf, spec_send, near_sig, near_tap, near_conv,
    work, sig_spec, tap_spec, send_sems, recv_sems, late,
):
    count = groups * shards
    rows = x_ref.shape[1]
    channels = w_out_ref.shape[0]
    half = shards // 2
    quarter = shards // 4
    lanes = rows // groups
    my_group = lax.axis_index("batch")
    my_shard = lax.axis_index("seq")
    me = my_group * shards + my_shard
    my_half = lax.div(my_shard, half)
    lower = my_half == 0
    upper = my_half == 1
    is_last = my_shard >= shards - quarter
    near_me = my_group * half + lax.rem(my_shard, half)
    barrier = pltpu.get_barrier_semaphore()

    def across(step):
        turn = step // groups
        shard = (1 - my_half) * half + turn // quarter * quarter + lax.rem(my_shard + turn, quarter)
        return (lax.rem(my_group + step, groups), shard)

    def level(step):
        turn = step // groups
        shard = lax.div(my_shard, quarter) * quarter + lax.rem(my_shard + turn, quarter)
        return (lax.rem(my_group + step, groups), shard)

    def beside(step):
        turn = step // groups
        plane = 2 * my_half + 1 - lax.rem(lax.div(my_shard, quarter), 2)
        return (lax.rem(my_group + step, groups), plane * quarter + lax.rem(my_shard + turn, quarter))

    wide = groups * quarter
    far_first = [across(step) for step in range(wide)]
    far_second = [across(step) for step in range(wide, 2 * wide)]
    far = far_first + far_second
    same_plane = [level(step) for step in range(1, wide)]
    next_plane = [beside(step) for step in range(wide)]
    near = next_plane + same_plane

    def signal(semaphore, peers):
        for group, shard in peers:
            pl.semaphore_signal(semaphore, inc=1, device_id=(group, shard), device_id_type=MESH)

    @pl.when(jnp.logical_not(is_last))
    def _():
        signal(barrier, far + near)

    @pl.when(is_last)
    def _():
        signal(barrier, same_plane)

    loads = [
        pltpu.make_async_copy(source, target, load_sems.at[n])
        for n, (source, target) in enumerate(
            (
                (x_hbm, x_ref),
                (w_in_hbm, w_in_ref),
                (taps_hbm, taps_ref),
                (w_out_hbm, w_out_ref),
                (cot_hbm, cot_ref),
                (twist_hbm, twist_ref),
                (high_hbm, high_ref),
                (low_hbm, low_ref),
            )
        )
    ]
    for load in loads:
        load.start()

    def push(source, target, slot, peers):
        for group, shard in peers:
            pltpu.make_async_remote_copy(
                src_ref=source.at[group * shards + shard],
                dst_ref=target.at[me],
                send_sem=send_sems.at[slot],
                recv_sem=recv_sems.at[slot],
                device_id=(group, shard),
                device_id_type=MESH,
            ).start()

    def push_taps(offsets):
        for offset in offsets:
            shard = lax.rem(my_shard + offset, shards)
            pltpu.make_async_remote_copy(
                src_ref=tap_send.at[my_group * shards + shard],
                dst_ref=tap_buf.at[my_shard],
                send_sem=send_sems.at[1],
                recv_sem=recv_sems.at[1],
                device_id=(my_group, shard),
                device_id_type=MESH,
            ).start()

    def bundle(source, target, slot, many):
        return pltpu.make_async_remote_copy(
            src_ref=source.at[pl.ds(0, many)],
            dst_ref=target.at[pl.ds(0, many)],
            send_sem=send_sems.at[slot],
            recv_sem=recv_sems.at[slot],
            device_id=(my_group, my_shard),
            device_id_type=MESH,
        )

    loads[0].wait()
    loads[1].wait()
    projected = lax.dot_general(
        w_in_ref[...], x_ref[0], (((0,), (1,)), ((), ())), preferred_element_type=jnp.float32
    )
    queries = projected[:channels]
    query_buf[...] = queries
    signal_part = projected[channels : 2 * channels] * projected[2 * channels :]
    sig_send[...] = signal_part.reshape(count, part, rows)
    loads[2].wait()
    tap_send[...] = taps_ref[...].T.reshape(count, part, rows)
    pl.semaphore_wait(barrier, jnp.where(is_last, count - 1, count - 1 - wide))

    @pl.when(is_last)
    def _():
        signal(late, far + next_plane)

    @pl.when(lower)
    def _():
        push(sig_send, sig_buf, 0, far_first + near)
        for group, shard in near:
            pltpu.make_async_remote_copy(
                src_ref=sig_send.at[group * shards + shard + half],
                dst_ref=near_sig.at[near_me],
                send_sem=send_sems.at[5],
                recv_sem=recv_sems.at[5],
                device_id=(group, shard),
                device_id_type=MESH,
            ).start()
        near_sig[near_me] = sig_send[me + half]
        for offset in range(1, half):
            shard = lax.rem(my_shard + offset, half)
            pltpu.make_async_remote_copy(
                src_ref=tap_send.at[my_group * shards + shard + half],
                dst_ref=near_tap.at[my_shard],
                send_sem=send_sems.at[6],
                recv_sem=recv_sems.at[6],
                device_id=(my_group, shard),
                device_id_type=MESH,
            ).start()
        near_tap[my_shard] = tap_send[me + half]

    @pl.when(upper)
    def _():
        push(sig_send, sig_buf, 0, far + same_plane)

    sig_buf[me] = sig_send[me]
    tap_buf[my_shard] = tap_send[me]
    loads[3].wait()
    loads[4].wait()
    back = lax.dot_general(
        w_out_ref[...], cot_ref[0], (((1,), (1,)), ((), ())), preferred_element_type=jnp.float32
    )
    cot_send[...] = (queries * back).reshape(count, part, rows)

    @pl.when(jnp.logical_not(is_last))
    def _():
        pl.semaphore_wait(late, wide)

    @pl.when(lower)
    def _():
        push(sig_send, sig_buf, 0, far_second)

    @pl.when(upper)
    def _():
        push(sig_send, sig_buf, 0, next_plane)

    @pl.when(upper)
    def _():
        push_taps(range(1, shards))

    push(cot_send, cot_buf, 2, far)

    @pl.when(lower)
    def _():
        push_taps(range(1, shards))

    push(cot_send, cot_buf, 2, near)
    cot_buf[me] = cot_send[me]

    def multiply(value):
        top = value.astype(jnp.bfloat16)
        rest = (value - top.astype(jnp.float32)).astype(jnp.bfloat16)
        high = high_ref[...]
        return (
            jnp.dot(top, high, preferred_element_type=jnp.float32)
            + jnp.dot(rest, high, preferred_element_type=jnp.float32)
            + jnp.dot(top, low_ref[...], preferred_element_type=jnp.float32)
        )

    for load in loads[5:]:
        load.wait()

    def forward(blocks, height):
        bands = len(blocks)
        turns = math.pi / bands
        for index in range(bands + 1):
            real_part = grouped_sum(
                blocks, [math.cos(turns * (a * index % (2 * bands))) for a in range(bands)]
            )
            imag_part = grouped_sum(
                blocks, [-math.sin(turns * (a * index % (2 * bands))) for a in range(bands)]
            )
            cos_t = twist_ref[0, index * (shards // bands)][None]
            sin_t = twist_ref[1, index * (shards // bands)][None]
            if imag_part is None:
                real_turned = real_part * cos_t
                imag_turned = -(real_part * sin_t)
            else:
                real_turned = real_part * cos_t + imag_part * sin_t
                imag_turned = imag_part * cos_t - real_part * sin_t
            place_at = pl.ds(index * height, height)
            work[place_at, :rows] = real_turned.reshape(height, rows)
            work[place_at, rows:] = imag_turned.reshape(height, rows)
        return multiply(work[pl.ds(0, (bands + 1) * height), :])

    height = groups * part

    def convolve(bands, target, stride):
        turns = math.pi / bands
        scale = 1.0 / (2 * bands * rows)
        used = pl.ds(0, (bands + 1) * height)
        for index in range(bands + 1):
            weight = scale if index in (0, bands) else 2.0 * scale
            tap_part = tap_spec[pl.ds(index * part, part), :] * weight
            real_tap = tap_part[None, :, :rows]
            imag_tap = tap_part[None, :, rows:]
            sig_part = sig_spec[pl.ds(index * height, height), :].reshape(groups, part, 2 * rows)
            real_sig = sig_part[:, :, :rows]
            imag_sig = sig_part[:, :, rows:]
            place_at = pl.ds(index * height, height)
            work[place_at, :rows] = (real_tap * real_sig - imag_tap * imag_sig).reshape(height, rows)
            work[place_at, rows:] = -(real_tap * imag_sig + imag_tap * real_sig).reshape(height, rows)
        work[used, :] = multiply(work[used, :])
        real_items = []
        imag_items = []
        for index in range(bands + 1):
            piece = work[pl.ds(index * height, height), :].reshape(groups, part, 2 * rows)
            cos_t = twist_ref[0, index * (shards // bands)][None]
            sin_t = twist_ref[1, index * (shards // bands)][None]
            real_items.append(piece[:, :, :rows] * cos_t + piece[:, :, rows:] * sin_t)
            imag_items.append(piece[:, :, :rows] * sin_t - piece[:, :, rows:] * cos_t)
        for a in range(bands):
            value = grouped_sum(
                real_items + imag_items,
                [math.cos(turns * (a * i % (2 * bands))) for i in range(bands + 1)]
                + [-math.sin(turns * (a * i % (2 * bands))) for i in range(bands + 1)],
            )
            for group in range(groups):
                target[group * stride + a] = value[group]

    @pl.when(lower)
    def _():
        bundle(sig_send, near_sig, 5, groups * half - 1).wait_recv()
        by_source = near_sig[...].reshape(groups, half, part, rows)
        sig_spec[pl.ds(0, (half + 1) * height), :] = forward(
            [by_source[:, a] for a in range(half)], height
        )
        bundle(tap_send, near_tap, 6, half - 1).wait_recv()
        tap_blocks = near_tap[...]
        tap_spec[pl.ds(0, (half + 1) * part), :] = forward(
            [tap_blocks[a][None] for a in range(half)], part
        )
        convolve(half, near_conv, half)
        for group, shard in near:
            pltpu.make_async_remote_copy(
                src_ref=near_conv.at[group * half + shard],
                dst_ref=conv_buf.at[me + half],
                send_sem=send_sems.at[7],
                recv_sem=recv_sems.at[3],
                device_id=(group, shard),
                device_id_type=MESH,
            ).start()
        conv_buf[me + half] = near_conv[near_me]

    bundle(sig_send, sig_buf, 0, count - 1).wait_recv()
    by_source = sig_buf[...].reshape(groups, shards, part, rows)
    sig_spec[...] = forward([by_source[:, a] for a in range(shards)], height)

    def respond():
        bundle(tap_send, tap_buf, 1, shards - 1).wait_recv()
        tap_blocks = tap_buf[...]
        tap_spec[...] = forward([tap_blocks[a][None] for a in range(shards)], part)
        convolve(shards, conv_send, shards)

    @pl.when(lower)
    def _():
        respond()
        push(conv_send, conv_buf, 3, far + near)
        conv_buf[me] = conv_send[me]

    factor = 1.0 / (2 * shards * rows)
    residues = shards + 1
    bundle(cot_send, cot_buf, 2, count - 1).wait_recv()
    by_source = cot_buf[...].reshape(groups, shards, part, rows)
    work[...] = forward([by_source[:, a] for a in range(shards)], height)
    real_spec = []
    imag_spec = []
    for index in range(residues):
        place_at = pl.ds(index * height, height)
        sig_part = (sig_spec[place_at, :] * factor).reshape(groups, part, 2 * rows)
        cot_part = work[place_at, :].reshape(groups, part, 2 * rows)
        real_sig, imag_sig = sig_part[:, :, :rows], sig_part[:, :, rows:]
        real_cot, imag_cot = cot_part[:, :, :rows], cot_part[:, :, rows:]
        real_spec.append(jnp.sum(real_sig * real_cot + imag_sig * imag_cot, axis=0))
        imag_spec.append(jnp.sum(real_sig * imag_cot - imag_sig * real_cot, axis=0))
    row = lax.broadcasted_iota(jnp.int32, (rows, rows), 0)
    column = lax.broadcasted_iota(jnp.int32, (rows, rows), 1)
    reverse = jnp.where(row + column == rows - 1, 1.0, 0.0).astype(jnp.bfloat16)
    straight = jnp.concatenate(
        real_spec[1:shards] + [-piece for piece in imag_spec[1:shards]], axis=0
    )
    turned = None
    for _ in range(3):
        top = straight.astype(jnp.bfloat16)
        straight = straight - top.astype(jnp.float32)
        term = jnp.dot(top, reverse, preferred_element_type=jnp.float32)
        turned = term if turned is None else turned + term
    for index in range(shards - 1, 0, -1):
        low_row = (index - 1) * part
        real_spec.append(turned[low_row : low_row + part])
        low_row += (shards - 1) * part
        imag_spec.append(turned[low_row : low_row + part])
    for shard in range(shards):
        for group in range(groups):
            pieces = [
                spec[index][:, group * lanes : (group + 1) * lanes]
                for spec in (real_spec, imag_spec)
                for index in (2 * shard, 2 * shard + 1)
            ]
            spec_send[group * shards + shard] = jnp.concatenate(pieces, axis=1)
    push(spec_send, spec_out, 4, far + near)

    @pl.when(upper)
    def _():
        respond()
        push(conv_send, conv_buf, 3, near)
        conv_buf[me] = conv_send[me]

    own = pltpu.make_async_copy(spec_send.at[me], spec_out.at[me], store_sems.at[0])
    own.start()

    @pl.when(lower)
    def _():
        bundle(conv_send, conv_buf, 3, count - 2).wait_recv()

    @pl.when(upper)
    def _():
        bundle(conv_send, conv_buf, 3, count - 1).wait_recv()

    gated = (query_buf[...] * conv_buf[...].reshape(channels, rows)).astype(jnp.bfloat16)
    out_ref[0] = lax.dot_general(
        gated, w_out_ref[...], (((0,), (0,)), ((), ())), preferred_element_type=jnp.float32
    ).astype(jnp.bfloat16)

    store = pltpu.make_async_copy(out_ref, out_hbm, store_sems.at[1])
    store.start()
    bundle(sig_send, sig_buf, 0, count - 1).wait_send()
    bundle(tap_send, tap_buf, 1, shards - 1).wait_send()
    bundle(cot_send, cot_buf, 2, count - 1).wait_send()

    @pl.when(lower)
    def _():
        bundle(conv_send, conv_buf, 3, count - 1).wait_send()
        bundle(sig_send, near_sig, 5, groups * half - 1).wait_send()
        bundle(tap_send, near_tap, 6, half - 1).wait_send()
        bundle(near_conv, conv_buf, 7, groups * half - 1).wait_send()

    @pl.when(upper)
    def _():
        bundle(conv_send, conv_buf, 3, groups * half - 1).wait_send()

    bundle(spec_send, spec_out, 4, count - 1).wait_send()
    own.wait()
    store.wait()
    bundle(spec_send, spec_out, 4, count - 1).wait_recv()


def finish(raw_hbm, spec_hbm, out_hbm, grad_hbm, raw_buf, spec_buf, grad_buf, load_sems, store_sems):
    load_spec = pltpu.make_async_copy(spec_hbm, spec_buf, load_sems.at[0])
    load_raw = pltpu.make_async_copy(raw_hbm, raw_buf, load_sems.at[1])
    load_spec.start()
    load_raw.start()
    count, part, width = spec_buf.shape
    stores = []
    load_spec.wait()
    for kind in range(2):
        piece = spec_buf[:, :, kind * (width // 2) : (kind + 1) * (width // 2)]
        grad_buf[kind] = piece.reshape(count * part, width // 2).T.reshape(grad_buf.shape[1:])
        store = pltpu.make_async_copy(grad_buf.at[kind], grad_hbm.at[kind], store_sems.at[kind])
        store.start()
        stores.append(store)
        if kind == 0:
            load_raw.wait()
            store = pltpu.make_async_copy(raw_buf, out_hbm, store_sems.at[2])
            store.start()
            stores.append(store)
    for store in stores:
        store.wait()


def direct(sequences, filter_taps, w_in, w_out, grad_out):
    groups = lax.axis_size("batch")
    shards = lax.axis_size("seq")
    rows = sequences.shape[1]
    channels = w_out.shape[0]
    count = groups * shards
    part = channels // count
    freq_rows = 2 * shards
    residues = shards + 1
    lanes = rows // groups
    high, low, twist = wide_tables(rows, freq_rows)
    operands = (
        sequences, filter_taps, w_in, w_out, grad_out,
        jnp.asarray(high), jnp.asarray(low), jnp.asarray(twist),
    )
    chunk = pltpu.VMEM((count, part, rows), jnp.float32)
    height = groups * part
    anywhere = pl.BlockSpec(memory_space=pl.ANY)
    raw, spectra = pl.pallas_call(
        functools.partial(kernel, groups, shards, part),
        out_shape=(
            jax.ShapeDtypeStruct((1, rows, channels), jnp.bfloat16),
            jax.ShapeDtypeStruct((count, part, rows), jnp.float32),
        ),
        in_specs=[anywhere] * 8,
        out_specs=(anywhere, anywhere),
        scratch_shapes=[
            *(pltpu.VMEM(item.shape, item.dtype) for item in operands),
            pltpu.VMEM((1, rows, channels), jnp.bfloat16),
            pltpu.SemaphoreType.DMA((8,)),
            pltpu.SemaphoreType.DMA((2,)),
            pltpu.VMEM((channels, rows), jnp.float32),
            chunk,
            chunk,
            chunk,
            chunk,
            chunk,
            pltpu.VMEM((shards, part, rows), jnp.float32),
            chunk,
            chunk,
            chunk,
            pltpu.VMEM((count // 2, part, rows), jnp.float32),
            pltpu.VMEM((shards // 2, part, rows), jnp.float32),
            pltpu.VMEM((count // 2, part, rows), jnp.float32),
            pltpu.VMEM((residues * height, 2 * rows), jnp.float32),
            pltpu.VMEM((residues * height, 2 * rows), jnp.float32),
            pltpu.VMEM((residues * part, 2 * rows), jnp.float32),
            pltpu.SemaphoreType.DMA((8,)),
            pltpu.SemaphoreType.DMA((7,)),
            pltpu.SemaphoreType.REGULAR,
        ],
        compiler_params=pltpu.CompilerParams(collective_id=0, has_side_effects=True),
    )(*operands)
    return pl.pallas_call(
        finish,
        out_shape=(
            jax.ShapeDtypeStruct((1, rows, channels), jnp.bfloat16),
            jax.ShapeDtypeStruct((2, 2, lanes, channels), jnp.float32),
        ),
        in_specs=[anywhere] * 2,
        out_specs=(anywhere, anywhere),
        scratch_shapes=[
            pltpu.VMEM(raw.shape, raw.dtype),
            pltpu.VMEM(spectra.shape, spectra.dtype),
            pltpu.VMEM((2, 2, lanes, channels), jnp.float32),
            pltpu.SemaphoreType.DMA((2,)),
            pltpu.SemaphoreType.DMA((3,)),
        ],
    )(raw, spectra)


def body(sequences, filter_taps, w_in, w_out, grad_out):
    groups = lax.axis_size("batch")
    count = groups * lax.axis_size("seq")
    rows = sequences.shape[1]
    fits = (
        sequences.shape[0] == 1
        and w_out.shape[0] == FULL_TILE * count
        and lax.axis_size("seq") % 4 == 0
        and rows % 128 == 0
        and rows % groups == 0
        and 2 * (rows // groups) % 128 == 0
    )
    chosen = direct if fits else local
    return chosen(sequences, filter_taps, w_in, w_out, grad_out)


def solution(mesh):
    placed = (P("batch", "seq", None), P("seq", None), P(), P(), P("batch", "seq", None))
    return jax.shard_map(
        body,
        mesh=mesh,
        in_specs=placed,
        out_specs=(P("batch", "seq", None), P(None, "seq", "batch", None)),
        check_vma=False,
    )
```

```python
import functools
import math

import jax
import jax.numpy as jnp
import numpy as np
from jax import lax
from jax.experimental import pallas as pl
from jax.experimental.pallas import tpu as pltpu
from jax.sharding import PartitionSpec as P

precise = lax.Precision.HIGHEST


def counting(length):
    return jnp.arange(length, dtype=jnp.int32)


def phase_table(left_index, right_index, period):
    product = left_index[:, None] * right_index[None, :] % period
    angles = product.astype(jnp.float32) * (2.0 * math.pi / period)
    return (jnp.cos(angles), jnp.sin(angles))


def split_length(length):
    outer_len = math.isqrt(length)
    while length % outer_len:
        outer_len -= 1
    return (outer_len, length // outer_len)


def local_forward(spectrum):
    groups = spectrum.shape[0]
    length = spectrum.shape[1]
    channels = spectrum.shape[3]
    outer_len, inner_len = split_length(length)
    shaped = spectrum.reshape(groups, outer_len, inner_len, 2, channels)
    real_in = shaped[:, :, :, 0]
    imag_in = shaped[:, :, :, 1]
    cos_outer, sin_outer = phase_table(counting(outer_len), counting(outer_len), outer_len)
    real_mid = jnp.einsum("jm,fmnc->fjnc", cos_outer, real_in, precision=precise) + jnp.einsum(
        "jm,fmnc->fjnc", sin_outer, imag_in, precision=precise
    )
    imag_mid = jnp.einsum("jm,fmnc->fjnc", cos_outer, imag_in, precision=precise) - jnp.einsum(
        "jm,fmnc->fjnc", sin_outer, real_in, precision=precise
    )
    cos_twist, sin_twist = phase_table(counting(outer_len), counting(inner_len), length)
    cos_twist = cos_twist[None, :, :, None]
    sin_twist = sin_twist[None, :, :, None]
    real_turned = real_mid * cos_twist + imag_mid * sin_twist
    imag_turned = imag_mid * cos_twist - real_mid * sin_twist
    cos_inner, sin_inner = phase_table(counting(inner_len), counting(inner_len), inner_len)
    real_out = jnp.einsum("kn,fjnc->fkjc", cos_inner, real_turned, precision=precise) + jnp.einsum(
        "kn,fjnc->fkjc", sin_inner, imag_turned, precision=precise
    )
    imag_out = jnp.einsum("kn,fjnc->fkjc", cos_inner, imag_turned, precision=precise) - jnp.einsum(
        "kn,fjnc->fkjc", sin_inner, real_turned, precision=precise
    )
    return jnp.stack([real_out, imag_out], axis=3).reshape(groups, length, 2, channels)


def local_inverse(real_spec, imag_spec):
    groups = real_spec.shape[0]
    length = real_spec.shape[1]
    channels = real_spec.shape[2]
    outer_len, inner_len = split_length(length)
    real_grid = real_spec.reshape(groups, inner_len, outer_len, channels)
    imag_grid = imag_spec.reshape(groups, inner_len, outer_len, channels)
    cos_inner, sin_inner = phase_table(counting(inner_len), counting(inner_len), inner_len)
    real_mid = jnp.einsum("nk,fkjc->fjnc", cos_inner, real_grid, precision=precise) - jnp.einsum(
        "nk,fkjc->fjnc", sin_inner, imag_grid, precision=precise
    )
    imag_mid = jnp.einsum("nk,fkjc->fjnc", cos_inner, imag_grid, precision=precise) + jnp.einsum(
        "nk,fkjc->fjnc", sin_inner, real_grid, precision=precise
    )
    cos_twist, sin_twist = phase_table(counting(outer_len), counting(inner_len), length)
    cos_twist = cos_twist[None, :, :, None]
    sin_twist = sin_twist[None, :, :, None]
    real_turned = real_mid * cos_twist - imag_mid * sin_twist
    imag_turned = imag_mid * cos_twist + real_mid * sin_twist
    cos_outer, sin_outer = phase_table(counting(outer_len), counting(outer_len), outer_len)
    real_out = jnp.einsum("mj,fjnc->fmnc", cos_outer, real_turned, precision=precise) - jnp.einsum(
        "mj,fjnc->fmnc", sin_outer, imag_turned, precision=precise
    )
    imag_out = jnp.einsum("mj,fjnc->fmnc", cos_outer, imag_turned, precision=precise) + jnp.einsum(
        "mj,fjnc->fmnc", sin_outer, real_turned, precision=precise
    )
    return (real_out.reshape(groups, length, channels), imag_out.reshape(groups, length, channels))


def forward_spectrum(columns, residue_order):
    shards = lax.axis_size("seq")
    local_len = columns.shape[0]
    block_rows = local_len // shards
    freq_rows = 2 * shards
    full_span = freq_rows * local_len
    glob_rows = lax.axis_index("seq") * block_rows + counting(block_rows)
    pieces = lax.all_to_all(columns[None], "seq", split_axis=1, concat_axis=0, tiled=True)
    cos_first, sin_first = phase_table(residue_order, counting(shards), freq_rows)
    real_part = jnp.einsum("ka,amc->kmc", cos_first, pieces[:, :, 0], precision=precise)
    imag_part = -jnp.einsum("ka,amc->kmc", sin_first, pieces[:, :, 0], precision=precise)
    cos_twist, sin_twist = phase_table(residue_order, glob_rows, full_span)
    cos_twist = cos_twist[:, :, None]
    sin_twist = sin_twist[:, :, None]
    real_turned = real_part * cos_twist + imag_part * sin_twist
    imag_turned = imag_part * cos_twist - real_part * sin_twist
    packed = jnp.stack([real_turned, imag_turned], axis=2)
    return local_forward(lax.all_to_all(packed, "seq", split_axis=0, concat_axis=1, tiled=True))


def inverse_signal(real_spec, imag_spec, residue_order):
    shards = lax.axis_size("seq")
    pair_rows = real_spec.shape[0]
    local_len = real_spec.shape[1]
    freq_rows = pair_rows * shards
    full_span = freq_rows * local_len
    real_part, imag_part = local_inverse(real_spec, imag_spec)
    pair_index = lax.dynamic_slice_in_dim(
        residue_order, lax.axis_index("seq") * pair_rows, pair_rows
    )
    cos_twist, sin_twist = phase_table(pair_index, counting(local_len), full_span)
    cos_twist = cos_twist[:, :, None]
    sin_twist = sin_twist[:, :, None]
    real_turned = real_part * cos_twist - imag_part * sin_twist
    imag_turned = imag_part * cos_twist + real_part * sin_twist
    packed = jnp.stack([real_turned, imag_turned], axis=2)
    pieces = lax.all_to_all(packed, "seq", split_axis=1, concat_axis=0, tiled=True)
    cos_last, sin_last = phase_table(counting(shards), residue_order, freq_rows)
    summed = jnp.einsum("ak,kmc->amc", cos_last, pieces[:, :, 0], precision=precise) - jnp.einsum(
        "ak,kmc->amc", sin_last, pieces[:, :, 1], precision=precise
    )
    columns = summed * (1.0 / full_span)
    placed = lax.all_to_all(columns, "seq", split_axis=0, concat_axis=1, tiled=True)
    return placed[0]


def local(sequences, filter_taps, w_in, w_out, grad_out):
    channels = w_out.shape[0]
    groups = lax.axis_size("batch")
    shards = lax.axis_size("seq")
    projected = jnp.dot(sequences[0], w_in, preferred_element_type=jnp.float32)
    queries = projected[:, :channels]
    signal = projected[:, channels : 2 * channels] * projected[:, 2 * channels :]
    back_grad = lax.dot_general(
        grad_out[0], w_out, (((1,), (1,)), ((), ())), preferred_element_type=jnp.float32
    )
    conv_grad = queries * back_grad
    order_table = np.arange(2 * shards)
    residue_order = jnp.asarray(order_table, jnp.int32)
    part_width = channels // groups
    filter_part = lax.dynamic_slice_in_dim(
        filter_taps, lax.axis_index("batch") * part_width, part_width, 1
    )
    signal_spec = forward_spectrum(signal[:, None], residue_order)
    grad_spec = forward_spectrum(conv_grad[:, None], residue_order)
    taps_spec = forward_spectrum(filter_part[:, None], residue_order)
    taps_spec = lax.all_gather(taps_spec, "batch", axis=3, tiled=True)
    real_sig = signal_spec[:, :, 0]
    imag_sig = signal_spec[:, :, 1]
    real_taps = taps_spec[:, :, 0]
    imag_taps = taps_spec[:, :, 1]
    real_conv = real_taps * real_sig - imag_taps * imag_sig
    imag_conv = real_taps * imag_sig + imag_taps * real_sig
    convolved = inverse_signal(real_conv, imag_conv, residue_order)
    gated = (queries * convolved).astype(jnp.bfloat16)
    layer_out = jnp.dot(gated, w_out, preferred_element_type=jnp.float32).astype(jnp.bfloat16)
    factor = 1.0 / (signal_spec.shape[0] * shards * signal_spec.shape[1])
    real_grad = grad_spec[:, :, 0]
    imag_grad = grad_spec[:, :, 1]
    grad_terms = jnp.stack(
        [
            (real_sig * real_grad + imag_sig * imag_grad) * factor,
            (real_sig * imag_grad - imag_sig * real_grad) * factor,
        ],
        axis=0,
    )
    filter_grad = lax.psum_scatter(grad_terms, "batch", scatter_dimension=2, tiled=True)
    return (layer_out[None], filter_grad)


MESH = pl.DeviceIdType.MESH
FULL_TILE = 8


def wide_tables(block_rows, freq_rows):
    residues = freq_rows // 2 + 1
    span = block_rows * freq_rows
    near = np.arange(block_rows)
    angles = 2.0 * np.pi * (np.outer(near, near) % block_rows) / block_rows
    cos_part, sin_part = np.cos(angles), np.sin(angles)
    matrix = np.block([[cos_part, -sin_part], [sin_part, cos_part]])
    high = matrix.astype(jnp.bfloat16)
    low = (matrix - high.astype(np.float64)).astype(jnp.bfloat16)
    twist_angles = 2.0 * np.pi * np.outer(np.arange(residues), near) / span
    twist = np.stack([np.cos(twist_angles), np.sin(twist_angles)], axis=0).astype(np.float32)
    twist = np.ascontiguousarray(
        np.broadcast_to(twist[:, :, None, :], (2, residues, FULL_TILE, block_rows))
    )
    return (high, low, twist)


def grouped_sum(items, weights):
    groups = {}
    for item, weight in zip(items, weights):
        size = round(abs(weight), 12)
        if size == 0.0:
            continue
        positive, total = groups.get(size, (None, None))
        if total is None:
            groups[size] = (weight > 0, item)
        elif positive == (weight > 0):
            groups[size] = (positive, total + item)
        else:
            groups[size] = (positive, total - item)
    result = None
    for size in sorted(groups, reverse=True):
        positive, total = groups[size]
        term = total if size == 1.0 else total * size
        if result is None:
            result = term if positive else -term
        else:
            result = result + term if positive else result - term
    return result


def kernel(
    groups, shards, part,
    x_hbm, taps_hbm, w_in_hbm, w_out_hbm, cot_hbm, high_hbm, low_hbm, twist_hbm,
    out_ref, spec_out,
    x_ref, taps_ref, w_in_ref, w_out_ref, cot_ref, high_ref, low_ref, twist_ref,
    load_sems, query_buf, sig_send, cot_send, tap_send, sig_buf, cot_buf, tap_buf,
    conv_send, conv_buf, spec_send, near_sig, near_tap, near_conv,
    work, sig_spec, tap_spec, send_sems, recv_sems, late,
):
    count = groups * shards
    rows = x_ref.shape[1]
    channels = w_out_ref.shape[0]
    half = shards // 2
    quarter = shards // 4
    lanes = rows // groups
    my_group = lax.axis_index("batch")
    my_shard = lax.axis_index("seq")
    me = my_group * shards + my_shard
    my_half = lax.div(my_shard, half)
    lower = my_half == 0
    upper = my_half == 1
    is_last = my_shard >= shards - quarter
    near_me = my_group * half + lax.rem(my_shard, half)
    barrier = pltpu.get_barrier_semaphore()

    def across(step):
        turn = step // groups
        shard = (1 - my_half) * half + turn // quarter * quarter + lax.rem(my_shard + turn, quarter)
        return (lax.rem(my_group + step, groups), shard)

    def level(step):
        turn = step // groups
        shard = lax.div(my_shard, quarter) * quarter + lax.rem(my_shard + turn, quarter)
        return (lax.rem(my_group + step, groups), shard)

    def beside(step):
        turn = step // groups
        plane = 2 * my_half + 1 - lax.rem(lax.div(my_shard, quarter), 2)
        return (lax.rem(my_group + step, groups), plane * quarter + lax.rem(my_shard + turn, quarter))

    wide = groups * quarter
    far_first = [across(step) for step in range(wide)]
    far_second = [across(step) for step in range(wide, 2 * wide)]
    far = far_first + far_second
    same_plane = [level(step) for step in range(1, wide)]
    next_plane = [beside(step) for step in range(wide)]
    near = next_plane + same_plane

    def signal(semaphore, peers):
        for group, shard in peers:
            pl.semaphore_signal(semaphore, inc=1, device_id=(group, shard), device_id_type=MESH)

    @pl.when(jnp.logical_not(is_last))
    def _():
        signal(barrier, far + near)

    @pl.when(is_last)
    def _():
        signal(barrier, same_plane)

    loads = [
        pltpu.make_async_copy(source, target, load_sems.at[n])
        for n, (source, target) in enumerate(
            (
                (x_hbm, x_ref),
                (w_in_hbm, w_in_ref),
                (taps_hbm, taps_ref),
                (w_out_hbm, w_out_ref),
                (cot_hbm, cot_ref),
                (twist_hbm, twist_ref),
                (high_hbm, high_ref),
                (low_hbm, low_ref),
            )
        )
    ]
    for load in loads:
        load.start()

    def push(source, target, slot, peers):
        for group, shard in peers:
            pltpu.make_async_remote_copy(
                src_ref=source.at[group * shards + shard],
                dst_ref=target.at[me],
                send_sem=send_sems.at[slot],
                recv_sem=recv_sems.at[slot],
                device_id=(group, shard),
                device_id_type=MESH,
            ).start()

    def push_taps(offsets):
        for offset in offsets:
            shard = lax.rem(my_shard + offset, shards)
            pltpu.make_async_remote_copy(
                src_ref=tap_send.at[my_group * shards + shard],
                dst_ref=tap_buf.at[my_shard],
                send_sem=send_sems.at[1],
                recv_sem=recv_sems.at[1],
                device_id=(my_group, shard),
                device_id_type=MESH,
            ).start()

    def bundle(source, target, slot, many):
        return pltpu.make_async_remote_copy(
            src_ref=source.at[pl.ds(0, many)],
            dst_ref=target.at[pl.ds(0, many)],
            send_sem=send_sems.at[slot],
            recv_sem=recv_sems.at[slot],
            device_id=(my_group, my_shard),
            device_id_type=MESH,
        )

    loads[0].wait()
    loads[1].wait()
    projected = lax.dot_general(
        w_in_ref[...], x_ref[0], (((0,), (1,)), ((), ())), preferred_element_type=jnp.float32
    )
    queries = projected[:channels]
    query_buf[...] = queries
    signal_part = projected[channels : 2 * channels] * projected[2 * channels :]
    sig_send[...] = signal_part.reshape(count, part, rows)
    loads[2].wait()
    tap_send[...] = taps_ref[...].T.reshape(count, part, rows)
    pl.semaphore_wait(barrier, jnp.where(is_last, count - 1, count - 1 - wide))

    @pl.when(is_last)
    def _():
        signal(late, far + next_plane)

    @pl.when(lower)
    def _():
        push(sig_send, sig_buf, 0, far_first + near)
        for group, shard in near:
            pltpu.make_async_remote_copy(
                src_ref=sig_send.at[group * shards + shard + half],
                dst_ref=near_sig.at[near_me],
                send_sem=send_sems.at[5],
                recv_sem=recv_sems.at[5],
                device_id=(group, shard),
                device_id_type=MESH,
            ).start()
        near_sig[near_me] = sig_send[me + half]
        for offset in range(1, half):
            shard = lax.rem(my_shard + offset, half)
            pltpu.make_async_remote_copy(
                src_ref=tap_send.at[my_group * shards + shard + half],
                dst_ref=near_tap.at[my_shard],
                send_sem=send_sems.at[6],
                recv_sem=recv_sems.at[6],
                device_id=(my_group, shard),
                device_id_type=MESH,
            ).start()
        near_tap[my_shard] = tap_send[me + half]

    @pl.when(upper)
    def _():
        push(sig_send, sig_buf, 0, far + same_plane)

    sig_buf[me] = sig_send[me]
    tap_buf[my_shard] = tap_send[me]
    loads[3].wait()
    loads[4].wait()
    back = lax.dot_general(
        w_out_ref[...], cot_ref[0], (((1,), (1,)), ((), ())), preferred_element_type=jnp.float32
    )
    cot_send[...] = (queries * back).reshape(count, part, rows)

    @pl.when(jnp.logical_not(is_last))
    def _():
        pl.semaphore_wait(late, wide)

    @pl.when(lower)
    def _():
        push(sig_send, sig_buf, 0, far_second)

    @pl.when(upper)
    def _():
        push(sig_send, sig_buf, 0, next_plane)

    @pl.when(upper)
    def _():
        push_taps(range(1, shards))

    push(cot_send, cot_buf, 2, far)

    @pl.when(lower)
    def _():
        push_taps(range(1, shards))

    push(cot_send, cot_buf, 2, near)
    cot_buf[me] = cot_send[me]

    def multiply(value):
        top = value.astype(jnp.bfloat16)
        rest = (value - top.astype(jnp.float32)).astype(jnp.bfloat16)
        high = high_ref[...]
        return (
            jnp.dot(top, high, preferred_element_type=jnp.float32)
            + jnp.dot(rest, high, preferred_element_type=jnp.float32)
            + jnp.dot(top, low_ref[...], preferred_element_type=jnp.float32)
        )

    for load in loads[5:]:
        load.wait()

    def forward(blocks, height):
        bands = len(blocks)
        turns = math.pi / bands
        for index in range(bands + 1):
            real_part = grouped_sum(
                blocks, [math.cos(turns * (a * index % (2 * bands))) for a in range(bands)]
            )
            imag_part = grouped_sum(
                blocks, [-math.sin(turns * (a * index % (2 * bands))) for a in range(bands)]
            )
            cos_t = twist_ref[0, index * (shards // bands)][None]
            sin_t = twist_ref[1, index * (shards // bands)][None]
            if imag_part is None:
                real_turned = real_part * cos_t
                imag_turned = -(real_part * sin_t)
            else:
                real_turned = real_part * cos_t + imag_part * sin_t
                imag_turned = imag_part * cos_t - real_part * sin_t
            place_at = pl.ds(index * height, height)
            work[place_at, :rows] = real_turned.reshape(height, rows)
            work[place_at, rows:] = imag_turned.reshape(height, rows)
        return multiply(work[pl.ds(0, (bands + 1) * height), :])

    height = groups * part

    def convolve(bands, target, stride):
        turns = math.pi / bands
        scale = 1.0 / (2 * bands * rows)
        used = pl.ds(0, (bands + 1) * height)
        for index in range(bands + 1):
            weight = scale if index in (0, bands) else 2.0 * scale
            tap_part = tap_spec[pl.ds(index * part, part), :] * weight
            real_tap = tap_part[None, :, :rows]
            imag_tap = tap_part[None, :, rows:]
            sig_part = sig_spec[pl.ds(index * height, height), :].reshape(groups, part, 2 * rows)
            real_sig = sig_part[:, :, :rows]
            imag_sig = sig_part[:, :, rows:]
            place_at = pl.ds(index * height, height)
            work[place_at, :rows] = (real_tap * real_sig - imag_tap * imag_sig).reshape(height, rows)
            work[place_at, rows:] = -(real_tap * imag_sig + imag_tap * real_sig).reshape(height, rows)
        work[used, :] = multiply(work[used, :])
        real_items = []
        imag_items = []
        for index in range(bands + 1):
            piece = work[pl.ds(index * height, height), :].reshape(groups, part, 2 * rows)
            cos_t = twist_ref[0, index * (shards // bands)][None]
            sin_t = twist_ref[1, index * (shards // bands)][None]
            real_items.append(piece[:, :, :rows] * cos_t + piece[:, :, rows:] * sin_t)
            imag_items.append(piece[:, :, :rows] * sin_t - piece[:, :, rows:] * cos_t)
        for a in range(bands):
            value = grouped_sum(
                real_items + imag_items,
                [math.cos(turns * (a * i % (2 * bands))) for i in range(bands + 1)]
                + [-math.sin(turns * (a * i % (2 * bands))) for i in range(bands + 1)],
            )
            for group in range(groups):
                target[group * stride + a] = value[group]

    @pl.when(lower)
    def _():
        bundle(sig_send, near_sig, 5, groups * half - 1).wait_recv()
        by_source = near_sig[...].reshape(groups, half, part, rows)
        sig_spec[pl.ds(0, (half + 1) * height), :] = forward(
            [by_source[:, a] for a in range(half)], height
        )
        bundle(tap_send, near_tap, 6, half - 1).wait_recv()
        tap_blocks = near_tap[...]
        tap_spec[pl.ds(0, (half + 1) * part), :] = forward(
            [tap_blocks[a][None] for a in range(half)], part
        )
        convolve(half, near_conv, half)
        for group, shard in near:
            pltpu.make_async_remote_copy(
                src_ref=near_conv.at[group * half + shard],
                dst_ref=conv_buf.at[me + half],
                send_sem=send_sems.at[7],
                recv_sem=recv_sems.at[3],
                device_id=(group, shard),
                device_id_type=MESH,
            ).start()
        conv_buf[me + half] = near_conv[near_me]

    bundle(sig_send, sig_buf, 0, count - 1).wait_recv()
    by_source = sig_buf[...].reshape(groups, shards, part, rows)
    sig_spec[...] = forward([by_source[:, a] for a in range(shards)], height)

    def respond():
        bundle(tap_send, tap_buf, 1, shards - 1).wait_recv()
        tap_blocks = tap_buf[...]
        tap_spec[...] = forward([tap_blocks[a][None] for a in range(shards)], part)
        convolve(shards, conv_send, shards)

    @pl.when(lower)
    def _():
        respond()
        push(conv_send, conv_buf, 3, far + near)
        conv_buf[me] = conv_send[me]

    factor = 1.0 / (2 * shards * rows)
    residues = shards + 1
    bundle(cot_send, cot_buf, 2, count - 1).wait_recv()
    by_source = cot_buf[...].reshape(groups, shards, part, rows)
    work[...] = forward([by_source[:, a] for a in range(shards)], height)
    real_spec = []
    imag_spec = []
    for index in range(residues):
        place_at = pl.ds(index * height, height)
        sig_part = (sig_spec[place_at, :] * factor).reshape(groups, part, 2 * rows)
        cot_part = work[place_at, :].reshape(groups, part, 2 * rows)
        real_sig, imag_sig = sig_part[:, :, :rows], sig_part[:, :, rows:]
        real_cot, imag_cot = cot_part[:, :, :rows], cot_part[:, :, rows:]
        real_spec.append(jnp.sum(real_sig * real_cot + imag_sig * imag_cot, axis=0))
        imag_spec.append(jnp.sum(real_sig * imag_cot - imag_sig * real_cot, axis=0))
    row = lax.broadcasted_iota(jnp.int32, (rows, rows), 0)
    column = lax.broadcasted_iota(jnp.int32, (rows, rows), 1)
    reverse = jnp.where(row + column == rows - 1, 1.0, 0.0).astype(jnp.bfloat16)
    straight = jnp.concatenate(
        real_spec[1:shards] + [-piece for piece in imag_spec[1:shards]], axis=0
    )
    turned = None
    for _ in range(3):
        top = straight.astype(jnp.bfloat16)
        straight = straight - top.astype(jnp.float32)
        term = jnp.dot(top, reverse, preferred_element_type=jnp.float32)
        turned = term if turned is None else turned + term
    for index in range(shards - 1, 0, -1):
        low_row = (index - 1) * part
        real_spec.append(turned[low_row : low_row + part])
        low_row += (shards - 1) * part
        imag_spec.append(turned[low_row : low_row + part])
    for shard in range(shards):
        for group in range(groups):
            pieces = [
                spec[index][:, group * lanes : (group + 1) * lanes]
                for spec in (real_spec, imag_spec)
                for index in (2 * shard, 2 * shard + 1)
            ]
            spec_send[group * shards + shard] = jnp.concatenate(pieces, axis=1)
    push(spec_send, spec_out, 4, far + near)

    @pl.when(upper)
    def _():
        respond()
        push(conv_send, conv_buf, 3, near)
        conv_buf[me] = conv_send[me]

    spec_out[me] = spec_send[me]

    @pl.when(lower)
    def _():
        bundle(conv_send, conv_buf, 3, count - 2).wait_recv()

    @pl.when(upper)
    def _():
        bundle(conv_send, conv_buf, 3, count - 1).wait_recv()

    gated = (query_buf[...] * conv_buf[...].reshape(channels, rows)).astype(jnp.bfloat16)
    out_ref[0] = lax.dot_general(
        gated, w_out_ref[...], (((0,), (0,)), ((), ())), preferred_element_type=jnp.float32
    ).astype(jnp.bfloat16)

    bundle(sig_send, sig_buf, 0, count - 1).wait_send()
    bundle(tap_send, tap_buf, 1, shards - 1).wait_send()
    bundle(cot_send, cot_buf, 2, count - 1).wait_send()

    @pl.when(lower)
    def _():
        bundle(conv_send, conv_buf, 3, count - 1).wait_send()
        bundle(sig_send, near_sig, 5, groups * half - 1).wait_send()
        bundle(tap_send, near_tap, 6, half - 1).wait_send()
        bundle(near_conv, conv_buf, 7, groups * half - 1).wait_send()

    @pl.when(upper)
    def _():
        bundle(conv_send, conv_buf, 3, groups * half - 1).wait_send()

    bundle(spec_send, spec_out, 4, count - 1).wait_send()
    bundle(spec_send, spec_out, 4, count - 1).wait_recv()


def finish(raw_buf, spec_buf, out_hbm, grad_hbm, grad_buf, store_sems):
    stores = [pltpu.make_async_copy(raw_buf, out_hbm, store_sems.at[2])]
    stores[0].start()
    count, part, width = spec_buf.shape
    for kind in range(2):
        piece = spec_buf[:, :, kind * (width // 2) : (kind + 1) * (width // 2)]
        grad_buf[kind] = piece.reshape(count * part, width // 2).T.reshape(grad_buf.shape[1:])
        store = pltpu.make_async_copy(grad_buf.at[kind], grad_hbm.at[kind], store_sems.at[kind])
        store.start()
        stores.append(store)
    for store in stores:
        store.wait()


def direct(sequences, filter_taps, w_in, w_out, grad_out):
    groups = lax.axis_size("batch")
    shards = lax.axis_size("seq")
    rows = sequences.shape[1]
    channels = w_out.shape[0]
    count = groups * shards
    part = channels // count
    freq_rows = 2 * shards
    residues = shards + 1
    lanes = rows // groups
    high, low, twist = wide_tables(rows, freq_rows)
    operands = (
        sequences, filter_taps, w_in, w_out, grad_out,
        jnp.asarray(high), jnp.asarray(low), jnp.asarray(twist),
    )
    chunk = pltpu.VMEM((count, part, rows), jnp.float32)
    height = groups * part
    anywhere = pl.BlockSpec(memory_space=pl.ANY)
    on_chip = pl.BlockSpec(memory_space=pltpu.VMEM)
    raw, spectra = pl.pallas_call(
        functools.partial(kernel, groups, shards, part),
        out_shape=(
            pltpu.VMEM((1, rows, channels), jnp.bfloat16),
            pltpu.VMEM((count, part, rows), jnp.float32),
        ),
        in_specs=[anywhere] * 8,
        out_specs=(on_chip, on_chip),
        scratch_shapes=[
            *(pltpu.VMEM(item.shape, item.dtype) for item in operands),
            pltpu.SemaphoreType.DMA((8,)),
            pltpu.VMEM((channels, rows), jnp.float32),
            chunk,
            chunk,
            chunk,
            chunk,
            chunk,
            pltpu.VMEM((shards, part, rows), jnp.float32),
            chunk,
            chunk,
            chunk,
            pltpu.VMEM((count // 2, part, rows), jnp.float32),
            pltpu.VMEM((shards // 2, part, rows), jnp.float32),
            pltpu.VMEM((count // 2, part, rows), jnp.float32),
            pltpu.VMEM((residues * height, 2 * rows), jnp.float32),
            pltpu.VMEM((residues * height, 2 * rows), jnp.float32),
            pltpu.VMEM((residues * part, 2 * rows), jnp.float32),
            pltpu.SemaphoreType.DMA((8,)),
            pltpu.SemaphoreType.DMA((7,)),
            pltpu.SemaphoreType.REGULAR,
        ],
        compiler_params=pltpu.CompilerParams(collective_id=0, has_side_effects=True),
    )(*operands)
    return pl.pallas_call(
        finish,
        out_shape=(
            jax.ShapeDtypeStruct((1, rows, channels), jnp.bfloat16),
            jax.ShapeDtypeStruct((2, 2, lanes, channels), jnp.float32),
        ),
        in_specs=[on_chip] * 2,
        out_specs=(anywhere, anywhere),
        scratch_shapes=[
            pltpu.VMEM((2, 2, lanes, channels), jnp.float32),
            pltpu.SemaphoreType.DMA((3,)),
        ],
    )(
        pltpu.with_memory_space_constraint(raw, pltpu.VMEM),
        pltpu.with_memory_space_constraint(spectra, pltpu.VMEM),
    )


def body(sequences, filter_taps, w_in, w_out, grad_out):
    groups = lax.axis_size("batch")
    count = groups * lax.axis_size("seq")
    rows = sequences.shape[1]
    fits = (
        sequences.shape[0] == 1
        and w_out.shape[0] == FULL_TILE * count
        and lax.axis_size("seq") % 4 == 0
        and rows % 128 == 0
        and rows % groups == 0
        and 2 * (rows // groups) % 128 == 0
    )
    chosen = direct if fits else local
    return chosen(sequences, filter_taps, w_in, w_out, grad_out)


def solution(mesh):
    placed = (P("batch", "seq", None), P("seq", None), P(), P(), P("batch", "seq", None))
    return jax.shard_map(
        body,
        mesh=mesh,
        in_specs=placed,
        out_specs=(P("batch", "seq", None), P(None, "seq", "batch", None)),
        check_vma=False,
    )
```

```python
import functools
import math

import jax
import jax.numpy as jnp
import numpy as np
from jax import lax
from jax.experimental import pallas as pl
from jax.experimental.pallas import tpu as pltpu
from jax.sharding import PartitionSpec as P

precise = lax.Precision.HIGHEST


def counting(length):
    return jnp.arange(length, dtype=jnp.int32)


def phase_table(left_index, right_index, period):
    product = left_index[:, None] * right_index[None, :] % period
    angles = product.astype(jnp.float32) * (2.0 * math.pi / period)
    return (jnp.cos(angles), jnp.sin(angles))


def split_length(length):
    outer_len = math.isqrt(length)
    while length % outer_len:
        outer_len -= 1
    return (outer_len, length // outer_len)


def local_forward(spectrum):
    groups = spectrum.shape[0]
    length = spectrum.shape[1]
    channels = spectrum.shape[3]
    outer_len, inner_len = split_length(length)
    shaped = spectrum.reshape(groups, outer_len, inner_len, 2, channels)
    real_in = shaped[:, :, :, 0]
    imag_in = shaped[:, :, :, 1]
    cos_outer, sin_outer = phase_table(counting(outer_len), counting(outer_len), outer_len)
    real_mid = jnp.einsum("jm,fmnc->fjnc", cos_outer, real_in, precision=precise) + jnp.einsum(
        "jm,fmnc->fjnc", sin_outer, imag_in, precision=precise
    )
    imag_mid = jnp.einsum("jm,fmnc->fjnc", cos_outer, imag_in, precision=precise) - jnp.einsum(
        "jm,fmnc->fjnc", sin_outer, real_in, precision=precise
    )
    cos_twist, sin_twist = phase_table(counting(outer_len), counting(inner_len), length)
    cos_twist = cos_twist[None, :, :, None]
    sin_twist = sin_twist[None, :, :, None]
    real_turned = real_mid * cos_twist + imag_mid * sin_twist
    imag_turned = imag_mid * cos_twist - real_mid * sin_twist
    cos_inner, sin_inner = phase_table(counting(inner_len), counting(inner_len), inner_len)
    real_out = jnp.einsum("kn,fjnc->fkjc", cos_inner, real_turned, precision=precise) + jnp.einsum(
        "kn,fjnc->fkjc", sin_inner, imag_turned, precision=precise
    )
    imag_out = jnp.einsum("kn,fjnc->fkjc", cos_inner, imag_turned, precision=precise) - jnp.einsum(
        "kn,fjnc->fkjc", sin_inner, real_turned, precision=precise
    )
    return jnp.stack([real_out, imag_out], axis=3).reshape(groups, length, 2, channels)


def local_inverse(real_spec, imag_spec):
    groups = real_spec.shape[0]
    length = real_spec.shape[1]
    channels = real_spec.shape[2]
    outer_len, inner_len = split_length(length)
    real_grid = real_spec.reshape(groups, inner_len, outer_len, channels)
    imag_grid = imag_spec.reshape(groups, inner_len, outer_len, channels)
    cos_inner, sin_inner = phase_table(counting(inner_len), counting(inner_len), inner_len)
    real_mid = jnp.einsum("nk,fkjc->fjnc", cos_inner, real_grid, precision=precise) - jnp.einsum(
        "nk,fkjc->fjnc", sin_inner, imag_grid, precision=precise
    )
    imag_mid = jnp.einsum("nk,fkjc->fjnc", cos_inner, imag_grid, precision=precise) + jnp.einsum(
        "nk,fkjc->fjnc", sin_inner, real_grid, precision=precise
    )
    cos_twist, sin_twist = phase_table(counting(outer_len), counting(inner_len), length)
    cos_twist = cos_twist[None, :, :, None]
    sin_twist = sin_twist[None, :, :, None]
    real_turned = real_mid * cos_twist - imag_mid * sin_twist
    imag_turned = imag_mid * cos_twist + real_mid * sin_twist
    cos_outer, sin_outer = phase_table(counting(outer_len), counting(outer_len), outer_len)
    real_out = jnp.einsum("mj,fjnc->fmnc", cos_outer, real_turned, precision=precise) - jnp.einsum(
        "mj,fjnc->fmnc", sin_outer, imag_turned, precision=precise
    )
    imag_out = jnp.einsum("mj,fjnc->fmnc", cos_outer, imag_turned, precision=precise) + jnp.einsum(
        "mj,fjnc->fmnc", sin_outer, real_turned, precision=precise
    )
    return (real_out.reshape(groups, length, channels), imag_out.reshape(groups, length, channels))


def forward_spectrum(columns, residue_order):
    shards = lax.axis_size("seq")
    local_len = columns.shape[0]
    block_rows = local_len // shards
    freq_rows = 2 * shards
    full_span = freq_rows * local_len
    glob_rows = lax.axis_index("seq") * block_rows + counting(block_rows)
    pieces = lax.all_to_all(columns[None], "seq", split_axis=1, concat_axis=0, tiled=True)
    cos_first, sin_first = phase_table(residue_order, counting(shards), freq_rows)
    real_part = jnp.einsum("ka,amc->kmc", cos_first, pieces[:, :, 0], precision=precise)
    imag_part = -jnp.einsum("ka,amc->kmc", sin_first, pieces[:, :, 0], precision=precise)
    cos_twist, sin_twist = phase_table(residue_order, glob_rows, full_span)
    cos_twist = cos_twist[:, :, None]
    sin_twist = sin_twist[:, :, None]
    real_turned = real_part * cos_twist + imag_part * sin_twist
    imag_turned = imag_part * cos_twist - real_part * sin_twist
    packed = jnp.stack([real_turned, imag_turned], axis=2)
    return local_forward(lax.all_to_all(packed, "seq", split_axis=0, concat_axis=1, tiled=True))


def inverse_signal(real_spec, imag_spec, residue_order):
    shards = lax.axis_size("seq")
    pair_rows = real_spec.shape[0]
    local_len = real_spec.shape[1]
    freq_rows = pair_rows * shards
    full_span = freq_rows * local_len
    real_part, imag_part = local_inverse(real_spec, imag_spec)
    pair_index = lax.dynamic_slice_in_dim(
        residue_order, lax.axis_index("seq") * pair_rows, pair_rows
    )
    cos_twist, sin_twist = phase_table(pair_index, counting(local_len), full_span)
    cos_twist = cos_twist[:, :, None]
    sin_twist = sin_twist[:, :, None]
    real_turned = real_part * cos_twist - imag_part * sin_twist
    imag_turned = imag_part * cos_twist + real_part * sin_twist
    packed = jnp.stack([real_turned, imag_turned], axis=2)
    pieces = lax.all_to_all(packed, "seq", split_axis=1, concat_axis=0, tiled=True)
    cos_last, sin_last = phase_table(counting(shards), residue_order, freq_rows)
    summed = jnp.einsum("ak,kmc->amc", cos_last, pieces[:, :, 0], precision=precise) - jnp.einsum(
        "ak,kmc->amc", sin_last, pieces[:, :, 1], precision=precise
    )
    columns = summed * (1.0 / full_span)
    placed = lax.all_to_all(columns, "seq", split_axis=0, concat_axis=1, tiled=True)
    return placed[0]


def local(sequences, filter_taps, w_in, w_out, grad_out):
    channels = w_out.shape[0]
    groups = lax.axis_size("batch")
    shards = lax.axis_size("seq")
    projected = jnp.dot(sequences[0], w_in, preferred_element_type=jnp.float32)
    queries = projected[:, :channels]
    signal = projected[:, channels : 2 * channels] * projected[:, 2 * channels :]
    back_grad = lax.dot_general(
        grad_out[0], w_out, (((1,), (1,)), ((), ())), preferred_element_type=jnp.float32
    )
    conv_grad = queries * back_grad
    order_table = np.arange(2 * shards)
    residue_order = jnp.asarray(order_table, jnp.int32)
    part_width = channels // groups
    filter_part = lax.dynamic_slice_in_dim(
        filter_taps, lax.axis_index("batch") * part_width, part_width, 1
    )
    signal_spec = forward_spectrum(signal[:, None], residue_order)
    grad_spec = forward_spectrum(conv_grad[:, None], residue_order)
    taps_spec = forward_spectrum(filter_part[:, None], residue_order)
    taps_spec = lax.all_gather(taps_spec, "batch", axis=3, tiled=True)
    real_sig = signal_spec[:, :, 0]
    imag_sig = signal_spec[:, :, 1]
    real_taps = taps_spec[:, :, 0]
    imag_taps = taps_spec[:, :, 1]
    real_conv = real_taps * real_sig - imag_taps * imag_sig
    imag_conv = real_taps * imag_sig + imag_taps * real_sig
    convolved = inverse_signal(real_conv, imag_conv, residue_order)
    gated = (queries * convolved).astype(jnp.bfloat16)
    layer_out = jnp.dot(gated, w_out, preferred_element_type=jnp.float32).astype(jnp.bfloat16)
    factor = 1.0 / (signal_spec.shape[0] * shards * signal_spec.shape[1])
    real_grad = grad_spec[:, :, 0]
    imag_grad = grad_spec[:, :, 1]
    grad_terms = jnp.stack(
        [
            (real_sig * real_grad + imag_sig * imag_grad) * factor,
            (real_sig * imag_grad - imag_sig * real_grad) * factor,
        ],
        axis=0,
    )
    filter_grad = lax.psum_scatter(grad_terms, "batch", scatter_dimension=2, tiled=True)
    return (layer_out[None], filter_grad)


MESH = pl.DeviceIdType.MESH
FULL_TILE = 8


def wide_tables(block_rows, freq_rows):
    residues = freq_rows // 2 + 1
    span = block_rows * freq_rows
    near = np.arange(block_rows)
    angles = 2.0 * np.pi * (np.outer(near, near) % block_rows) / block_rows
    cos_part, sin_part = np.cos(angles), np.sin(angles)
    matrix = np.block([[cos_part, -sin_part], [sin_part, cos_part]])
    high = matrix.astype(jnp.bfloat16)
    low = (matrix - high.astype(np.float64)).astype(jnp.bfloat16)
    twist_angles = 2.0 * np.pi * np.outer(np.arange(residues), near) / span
    twist = np.stack([np.cos(twist_angles), np.sin(twist_angles)], axis=0).astype(np.float32)
    twist = np.ascontiguousarray(
        np.broadcast_to(twist[:, :, None, :], (2, residues, FULL_TILE, block_rows))
    )
    return (high, low, twist)


def grouped_sum(items, weights):
    groups = {}
    for item, weight in zip(items, weights):
        size = round(abs(weight), 12)
        if size == 0.0:
            continue
        positive, total = groups.get(size, (None, None))
        if total is None:
            groups[size] = (weight > 0, item)
        elif positive == (weight > 0):
            groups[size] = (positive, total + item)
        else:
            groups[size] = (positive, total - item)
    result = None
    for size in sorted(groups, reverse=True):
        positive, total = groups[size]
        term = total if size == 1.0 else total * size
        if result is None:
            result = term if positive else -term
        else:
            result = result + term if positive else result - term
    return result


def kernel(
    groups, shards, part,
    x_hbm, taps_hbm, w_in_hbm, w_out_hbm, cot_hbm, high_hbm, low_hbm, twist_hbm,
    out_ref, spec_out,
    x_ref, taps_ref, w_in_ref, w_out_ref, cot_ref, high_ref, low_ref, twist_ref,
    load_sems, query_buf, sig_send, cot_send, tap_send, sig_buf, cot_buf, tap_buf,
    conv_send, conv_buf, spec_send, near_sig, near_tap, near_conv,
    work, sig_spec, tap_spec, near_sig_spec, near_tap_spec, send_sems, recv_sems, late,
):
    count = groups * shards
    rows = x_ref.shape[1]
    channels = w_out_ref.shape[0]
    half = shards // 2
    quarter = shards // 4
    lanes = rows // groups
    my_group = lax.axis_index("batch")
    my_shard = lax.axis_index("seq")
    me = my_group * shards + my_shard
    my_half = lax.div(my_shard, half)
    lower = my_half == 0
    upper = my_half == 1
    is_last = my_shard >= shards - quarter
    near_me = my_group * half + lax.rem(my_shard, half)
    barrier = pltpu.get_barrier_semaphore()

    def across(step):
        turn = step // groups
        shard = (1 - my_half) * half + turn // quarter * quarter + lax.rem(my_shard + turn, quarter)
        return (lax.rem(my_group + step, groups), shard)

    def level(step):
        turn = step // groups
        shard = lax.div(my_shard, quarter) * quarter + lax.rem(my_shard + turn, quarter)
        return (lax.rem(my_group + step, groups), shard)

    def beside(step):
        turn = step // groups
        plane = 2 * my_half + 1 - lax.rem(lax.div(my_shard, quarter), 2)
        return (lax.rem(my_group + step, groups), plane * quarter + lax.rem(my_shard + turn, quarter))

    wide = groups * quarter
    far_first = [across(step) for step in range(wide)]
    far_second = [across(step) for step in range(wide, 2 * wide)]
    far = far_first + far_second
    same_plane = [level(step) for step in range(1, wide)]
    next_plane = [beside(step) for step in range(wide)]
    near = next_plane + same_plane

    def signal(semaphore, peers):
        for group, shard in peers:
            pl.semaphore_signal(semaphore, inc=1, device_id=(group, shard), device_id_type=MESH)

    @pl.when(jnp.logical_not(is_last))
    def _():
        signal(barrier, far + near)

    @pl.when(is_last)
    def _():
        signal(barrier, same_plane)

    loads = [
        pltpu.make_async_copy(source, target, load_sems.at[n])
        for n, (source, target) in enumerate(
            (
                (x_hbm, x_ref),
                (w_in_hbm, w_in_ref),
                (taps_hbm, taps_ref),
                (w_out_hbm, w_out_ref),
                (cot_hbm, cot_ref),
                (twist_hbm, twist_ref),
                (high_hbm, high_ref),
                (low_hbm, low_ref),
            )
        )
    ]
    for load in loads:
        load.start()

    def push(source, target, slot, peers):
        for group, shard in peers:
            pltpu.make_async_remote_copy(
                src_ref=source.at[group * shards + shard],
                dst_ref=target.at[me],
                send_sem=send_sems.at[slot],
                recv_sem=recv_sems.at[slot],
                device_id=(group, shard),
                device_id_type=MESH,
            ).start()

    def push_taps(turns, opposite):
        base = (my_half + opposite - 2 * my_half * opposite) * half
        for turn in turns:
            shard = base + lax.rem(my_shard + turn, half)
            pltpu.make_async_remote_copy(
                src_ref=tap_send.at[my_group * shards + shard],
                dst_ref=tap_buf.at[my_shard],
                send_sem=send_sems.at[1],
                recv_sem=recv_sems.at[1],
                device_id=(my_group, shard),
                device_id_type=MESH,
            ).start()

    def bundle(source, target, slot, many):
        return pltpu.make_async_remote_copy(
            src_ref=source.at[pl.ds(0, many)],
            dst_ref=target.at[pl.ds(0, many)],
            send_sem=send_sems.at[slot],
            recv_sem=recv_sems.at[slot],
            device_id=(my_group, my_shard),
            device_id_type=MESH,
        )

    loads[0].wait()
    loads[1].wait()
    projected = lax.dot_general(
        w_in_ref[...], x_ref[0], (((0,), (1,)), ((), ())), preferred_element_type=jnp.float32
    )
    queries = projected[:channels]
    query_buf[...] = queries
    signal_part = projected[channels : 2 * channels] * projected[2 * channels :]
    sig_send[...] = signal_part.reshape(count, part, rows)
    loads[2].wait()
    tap_send[...] = taps_ref[...].T.reshape(count, part, rows)
    pl.semaphore_wait(barrier, jnp.where(is_last, count - 1, count - 1 - wide))

    @pl.when(is_last)
    def _():
        signal(late, far + next_plane)

    @pl.when(lower)
    def _():
        push(sig_send, sig_buf, 0, far_first + near)
        for group, shard in near:
            pltpu.make_async_remote_copy(
                src_ref=sig_send.at[group * shards + shard + half],
                dst_ref=near_sig.at[near_me],
                send_sem=send_sems.at[5],
                recv_sem=recv_sems.at[5],
                device_id=(group, shard),
                device_id_type=MESH,
            ).start()
        near_sig[near_me] = sig_send[me + half]
        for offset in range(1, half):
            shard = lax.rem(my_shard + offset, half)
            pltpu.make_async_remote_copy(
                src_ref=tap_send.at[my_group * shards + shard + half],
                dst_ref=near_tap.at[my_shard],
                send_sem=send_sems.at[6],
                recv_sem=recv_sems.at[6],
                device_id=(my_group, shard),
                device_id_type=MESH,
            ).start()
        near_tap[my_shard] = tap_send[me + half]

    @pl.when(upper)
    def _():
        push(sig_send, sig_buf, 0, far)
        push_taps(range(half), 1)
        push(sig_send, sig_buf, 0, same_plane)

    sig_buf[me] = sig_send[me]
    tap_buf[my_shard] = tap_send[me]
    loads[3].wait()
    loads[4].wait()
    back = lax.dot_general(
        w_out_ref[...], cot_ref[0], (((1,), (1,)), ((), ())), preferred_element_type=jnp.float32
    )
    cot_send[...] = (queries * back).reshape(count, part, rows)

    @pl.when(jnp.logical_not(is_last))
    def _():
        pl.semaphore_wait(late, wide)

    @pl.when(lower)
    def _():
        push(sig_send, sig_buf, 0, far_second)

    @pl.when(upper)
    def _():
        push(sig_send, sig_buf, 0, next_plane)

    @pl.when(lower)
    def _():
        push_taps(range(1, half), 0)

    push(cot_send, cot_buf, 2, far)

    @pl.when(lower)
    def _():
        push_taps(range(half), 1)

    push(cot_send, cot_buf, 2, near)

    @pl.when(upper)
    def _():
        push_taps(range(1, half), 0)

    cot_buf[me] = cot_send[me]

    def multiply(value):
        top = value.astype(jnp.bfloat16)
        rest = (value - top.astype(jnp.float32)).astype(jnp.bfloat16)
        high = high_ref[...]
        return (
            jnp.dot(top, high, preferred_element_type=jnp.float32)
            + jnp.dot(rest, high, preferred_element_type=jnp.float32)
            + jnp.dot(top, low_ref[...], preferred_element_type=jnp.float32)
        )

    for load in loads[5:]:
        load.wait()

    def forward(blocks, height):
        bands = len(blocks)
        turns = math.pi / bands
        for index in range(bands + 1):
            real_part = grouped_sum(
                blocks, [math.cos(turns * (a * index % (2 * bands))) for a in range(bands)]
            )
            imag_part = grouped_sum(
                blocks, [-math.sin(turns * (a * index % (2 * bands))) for a in range(bands)]
            )
            cos_t = twist_ref[0, index * (shards // bands)][None]
            sin_t = twist_ref[1, index * (shards // bands)][None]
            if imag_part is None:
                real_turned = real_part * cos_t
                imag_turned = -(real_part * sin_t)
            else:
                real_turned = real_part * cos_t + imag_part * sin_t
                imag_turned = imag_part * cos_t - real_part * sin_t
            place_at = pl.ds(index * height, height)
            work[place_at, :rows] = real_turned.reshape(height, rows)
            work[place_at, rows:] = imag_turned.reshape(height, rows)
        return multiply(work[pl.ds(0, (bands + 1) * height), :])

    height = groups * part

    def convolve(bands, sig_from, tap_from, target):
        turns = math.pi / bands
        scale = 1.0 / (2 * bands * rows)
        used = pl.ds(0, (bands + 1) * height)
        for index in range(bands + 1):
            weight = scale if index in (0, bands) else 2.0 * scale
            tap_part = tap_from[pl.ds(index * part, part), :] * weight
            real_tap = tap_part[None, :, :rows]
            imag_tap = tap_part[None, :, rows:]
            sig_part = sig_from[pl.ds(index * height, height), :].reshape(groups, part, 2 * rows)
            real_sig = sig_part[:, :, :rows]
            imag_sig = sig_part[:, :, rows:]
            place_at = pl.ds(index * height, height)
            work[place_at, :rows] = (real_tap * real_sig - imag_tap * imag_sig).reshape(height, rows)
            work[place_at, rows:] = -(real_tap * imag_sig + imag_tap * real_sig).reshape(height, rows)
        work[used, :] = multiply(work[used, :])
        real_items = []
        imag_items = []
        for index in range(bands + 1):
            piece = work[pl.ds(index * height, height), :].reshape(groups, part, 2 * rows)
            cos_t = twist_ref[0, index * (shards // bands)][None]
            sin_t = twist_ref[1, index * (shards // bands)][None]
            real_items.append(piece[:, :, :rows] * cos_t + piece[:, :, rows:] * sin_t)
            imag_items.append(piece[:, :, :rows] * sin_t - piece[:, :, rows:] * cos_t)
        for a in range(bands):
            value = grouped_sum(
                real_items + imag_items,
                [math.cos(turns * (a * i % (2 * bands))) for i in range(bands + 1)]
                + [-math.sin(turns * (a * i % (2 * bands))) for i in range(bands + 1)],
            )
            for group in range(groups):
                target[group * bands + a] = value[group]

    bundle(sig_send, sig_buf, 0, count - 1).wait_recv()
    by_source = sig_buf[...].reshape(groups, shards, part, rows)
    sig_spec[...] = forward([by_source[:, a] for a in range(shards)], height)

    def respond():
        bundle(tap_send, tap_buf, 1, shards - 1).wait_recv()
        tap_blocks = tap_buf[...]
        tap_spec[...] = forward([tap_blocks[a][None] for a in range(shards)], part)
        convolve(shards, sig_spec, tap_spec, conv_send)

    @pl.when(lower)
    def _():
        respond()
        push(conv_send, conv_buf, 3, far + near)
        conv_buf[me] = conv_send[me]

    @pl.when(lower)
    def _():
        bundle(sig_send, near_sig, 5, groups * half - 1).wait_recv()
        by_source = near_sig[...].reshape(groups, half, part, rows)
        near_sig_spec[...] = forward(
            [by_source[:, a] for a in range(half)], height
        )
        bundle(tap_send, near_tap, 6, half - 1).wait_recv()
        tap_blocks = near_tap[...]
        near_tap_spec[...] = forward(
            [tap_blocks[a][None] for a in range(half)], part
        )
        convolve(half, near_sig_spec, near_tap_spec, near_conv)
        for group, shard in near:
            pltpu.make_async_remote_copy(
                src_ref=near_conv.at[group * half + shard],
                dst_ref=conv_buf.at[me + half],
                send_sem=send_sems.at[7],
                recv_sem=recv_sems.at[3],
                device_id=(group, shard),
                device_id_type=MESH,
            ).start()
        conv_buf[me + half] = near_conv[near_me]

    factor = 1.0 / (2 * shards * rows)
    residues = shards + 1
    bundle(cot_send, cot_buf, 2, count - 1).wait_recv()
    by_source = cot_buf[...].reshape(groups, shards, part, rows)
    work[...] = forward([by_source[:, a] for a in range(shards)], height)
    real_spec = []
    imag_spec = []
    for index in range(residues):
        place_at = pl.ds(index * height, height)
        sig_part = (sig_spec[place_at, :] * factor).reshape(groups, part, 2 * rows)
        cot_part = work[place_at, :].reshape(groups, part, 2 * rows)
        real_sig, imag_sig = sig_part[:, :, :rows], sig_part[:, :, rows:]
        real_cot, imag_cot = cot_part[:, :, :rows], cot_part[:, :, rows:]
        real_spec.append(jnp.sum(real_sig * real_cot + imag_sig * imag_cot, axis=0))
        imag_spec.append(jnp.sum(real_sig * imag_cot - imag_sig * real_cot, axis=0))
    row = lax.broadcasted_iota(jnp.int32, (rows, rows), 0)
    column = lax.broadcasted_iota(jnp.int32, (rows, rows), 1)
    reverse = jnp.where(row + column == rows - 1, 1.0, 0.0).astype(jnp.bfloat16)
    straight = jnp.concatenate(
        real_spec[1:shards] + [-piece for piece in imag_spec[1:shards]], axis=0
    )
    turned = None
    for _ in range(3):
        top = straight.astype(jnp.bfloat16)
        straight = straight - top.astype(jnp.float32)
        term = jnp.dot(top, reverse, preferred_element_type=jnp.float32)
        turned = term if turned is None else turned + term
    for index in range(shards - 1, 0, -1):
        low_row = (index - 1) * part
        real_spec.append(turned[low_row : low_row + part])
        low_row += (shards - 1) * part
        imag_spec.append(turned[low_row : low_row + part])
    for shard in range(shards):
        for group in range(groups):
            pieces = [
                spec[index][:, group * lanes : (group + 1) * lanes]
                for spec in (real_spec, imag_spec)
                for index in (2 * shard, 2 * shard + 1)
            ]
            spec_send[group * shards + shard] = jnp.concatenate(pieces, axis=1)
    push(spec_send, spec_out, 4, far + near)

    @pl.when(upper)
    def _():
        respond()
        push(conv_send, conv_buf, 3, near)
        conv_buf[me] = conv_send[me]

    spec_out[me] = spec_send[me]

    @pl.when(lower)
    def _():
        bundle(conv_send, conv_buf, 3, count - 2).wait_recv()

    @pl.when(upper)
    def _():
        bundle(conv_send, conv_buf, 3, count - 1).wait_recv()

    gated = (query_buf[...] * conv_buf[...].reshape(channels, rows)).astype(jnp.bfloat16)
    out_ref[0] = lax.dot_general(
        gated, w_out_ref[...], (((0,), (0,)), ((), ())), preferred_element_type=jnp.float32
    ).astype(jnp.bfloat16)

    bundle(sig_send, sig_buf, 0, count - 1).wait_send()
    bundle(tap_send, tap_buf, 1, shards - 1).wait_send()
    bundle(cot_send, cot_buf, 2, count - 1).wait_send()

    @pl.when(lower)
    def _():
        bundle(conv_send, conv_buf, 3, count - 1).wait_send()
        bundle(sig_send, near_sig, 5, groups * half - 1).wait_send()
        bundle(tap_send, near_tap, 6, half - 1).wait_send()
        bundle(near_conv, conv_buf, 7, groups * half - 1).wait_send()

    @pl.when(upper)
    def _():
        bundle(conv_send, conv_buf, 3, groups * half - 1).wait_send()

    bundle(spec_send, spec_out, 4, count - 1).wait_send()
    bundle(spec_send, spec_out, 4, count - 1).wait_recv()


def finish(raw_buf, spec_buf, out_hbm, grad_hbm, grad_buf, store_sems):
    stores = [pltpu.make_async_copy(raw_buf, out_hbm, store_sems.at[2])]
    stores[0].start()
    count, part, width = spec_buf.shape
    for kind in range(2):
        piece = spec_buf[:, :, kind * (width // 2) : (kind + 1) * (width // 2)]
        grad_buf[kind] = piece.reshape(count * part, width // 2).T.reshape(grad_buf.shape[1:])
        store = pltpu.make_async_copy(grad_buf.at[kind], grad_hbm.at[kind], store_sems.at[kind])
        store.start()
        stores.append(store)
    for store in stores:
        store.wait()


def direct(sequences, filter_taps, w_in, w_out, grad_out):
    groups = lax.axis_size("batch")
    shards = lax.axis_size("seq")
    rows = sequences.shape[1]
    channels = w_out.shape[0]
    count = groups * shards
    part = channels // count
    freq_rows = 2 * shards
    residues = shards + 1
    lanes = rows // groups
    high, low, twist = wide_tables(rows, freq_rows)
    operands = (
        sequences, filter_taps, w_in, w_out, grad_out,
        jnp.asarray(high), jnp.asarray(low), jnp.asarray(twist),
    )
    chunk = pltpu.VMEM((count, part, rows), jnp.float32)
    height = groups * part
    anywhere = pl.BlockSpec(memory_space=pl.ANY)
    on_chip = pl.BlockSpec(memory_space=pltpu.VMEM)
    raw, spectra = pl.pallas_call(
        functools.partial(kernel, groups, shards, part),
        out_shape=(
            pltpu.VMEM((1, rows, channels), jnp.bfloat16),
            pltpu.VMEM((count, part, rows), jnp.float32),
        ),
        in_specs=[anywhere] * 8,
        out_specs=(on_chip, on_chip),
        scratch_shapes=[
            *(pltpu.VMEM(item.shape, item.dtype) for item in operands),
            pltpu.SemaphoreType.DMA((8,)),
            pltpu.VMEM((channels, rows), jnp.float32),
            chunk,
            chunk,
            chunk,
            chunk,
            chunk,
            pltpu.VMEM((shards, part, rows), jnp.float32),
            chunk,
            chunk,
            chunk,
            pltpu.VMEM((count // 2, part, rows), jnp.float32),
            pltpu.VMEM((shards // 2, part, rows), jnp.float32),
            pltpu.VMEM((count // 2, part, rows), jnp.float32),
            pltpu.VMEM((residues * height, 2 * rows), jnp.float32),
            pltpu.VMEM((residues * height, 2 * rows), jnp.float32),
            pltpu.VMEM((residues * part, 2 * rows), jnp.float32),
            pltpu.VMEM(((shards // 2 + 1) * height, 2 * rows), jnp.float32),
            pltpu.VMEM(((shards // 2 + 1) * part, 2 * rows), jnp.float32),
            pltpu.SemaphoreType.DMA((8,)),
            pltpu.SemaphoreType.DMA((7,)),
            pltpu.SemaphoreType.REGULAR,
        ],
        compiler_params=pltpu.CompilerParams(collective_id=0, has_side_effects=True),
    )(*operands)
    return pl.pallas_call(
        finish,
        out_shape=(
            jax.ShapeDtypeStruct((1, rows, channels), jnp.bfloat16),
            jax.ShapeDtypeStruct((2, 2, lanes, channels), jnp.float32),
        ),
        in_specs=[on_chip] * 2,
        out_specs=(anywhere, anywhere),
        scratch_shapes=[
            pltpu.VMEM((2, 2, lanes, channels), jnp.float32),
            pltpu.SemaphoreType.DMA((3,)),
        ],
    )(
        pltpu.with_memory_space_constraint(raw, pltpu.VMEM),
        pltpu.with_memory_space_constraint(spectra, pltpu.VMEM),
    )


def body(sequences, filter_taps, w_in, w_out, grad_out):
    groups = lax.axis_size("batch")
    count = groups * lax.axis_size("seq")
    rows = sequences.shape[1]
    fits = (
        sequences.shape[0] == 1
        and w_out.shape[0] == FULL_TILE * count
        and lax.axis_size("seq") % 4 == 0
        and rows % 128 == 0
        and rows % groups == 0
        and 2 * (rows // groups) % 128 == 0
    )
    chosen = direct if fits else local
    return chosen(sequences, filter_taps, w_in, w_out, grad_out)


def solution(mesh):
    placed = (P("batch", "seq", None), P("seq", None), P(), P(), P("batch", "seq", None))
    return jax.shard_map(
        body,
        mesh=mesh,
        in_specs=placed,
        out_specs=(P("batch", "seq", None), P(None, "seq", "batch", None)),
        check_vma=False,
    )
```

```python
import functools
import math

import jax
import jax.numpy as jnp
import numpy as np
from jax import lax
from jax.experimental import pallas as pl
from jax.experimental.pallas import tpu as pltpu
from jax.sharding import PartitionSpec as P

precise = lax.Precision.HIGHEST


def counting(length):
    return jnp.arange(length, dtype=jnp.int32)


def phase_table(left_index, right_index, period):
    product = left_index[:, None] * right_index[None, :] % period
    angles = product.astype(jnp.float32) * (2.0 * math.pi / period)
    return (jnp.cos(angles), jnp.sin(angles))


def split_length(length):
    outer_len = math.isqrt(length)
    while length % outer_len:
        outer_len -= 1
    return (outer_len, length // outer_len)


def local_forward(spectrum):
    groups = spectrum.shape[0]
    length = spectrum.shape[1]
    channels = spectrum.shape[3]
    outer_len, inner_len = split_length(length)
    shaped = spectrum.reshape(groups, outer_len, inner_len, 2, channels)
    real_in = shaped[:, :, :, 0]
    imag_in = shaped[:, :, :, 1]
    cos_outer, sin_outer = phase_table(counting(outer_len), counting(outer_len), outer_len)
    real_mid = jnp.einsum("jm,fmnc->fjnc", cos_outer, real_in, precision=precise) + jnp.einsum(
        "jm,fmnc->fjnc", sin_outer, imag_in, precision=precise
    )
    imag_mid = jnp.einsum("jm,fmnc->fjnc", cos_outer, imag_in, precision=precise) - jnp.einsum(
        "jm,fmnc->fjnc", sin_outer, real_in, precision=precise
    )
    cos_twist, sin_twist = phase_table(counting(outer_len), counting(inner_len), length)
    cos_twist = cos_twist[None, :, :, None]
    sin_twist = sin_twist[None, :, :, None]
    real_turned = real_mid * cos_twist + imag_mid * sin_twist
    imag_turned = imag_mid * cos_twist - real_mid * sin_twist
    cos_inner, sin_inner = phase_table(counting(inner_len), counting(inner_len), inner_len)
    real_out = jnp.einsum("kn,fjnc->fkjc", cos_inner, real_turned, precision=precise) + jnp.einsum(
        "kn,fjnc->fkjc", sin_inner, imag_turned, precision=precise
    )
    imag_out = jnp.einsum("kn,fjnc->fkjc", cos_inner, imag_turned, precision=precise) - jnp.einsum(
        "kn,fjnc->fkjc", sin_inner, real_turned, precision=precise
    )
    return jnp.stack([real_out, imag_out], axis=3).reshape(groups, length, 2, channels)


def local_inverse(real_spec, imag_spec):
    groups = real_spec.shape[0]
    length = real_spec.shape[1]
    channels = real_spec.shape[2]
    outer_len, inner_len = split_length(length)
    real_grid = real_spec.reshape(groups, inner_len, outer_len, channels)
    imag_grid = imag_spec.reshape(groups, inner_len, outer_len, channels)
    cos_inner, sin_inner = phase_table(counting(inner_len), counting(inner_len), inner_len)
    real_mid = jnp.einsum("nk,fkjc->fjnc", cos_inner, real_grid, precision=precise) - jnp.einsum(
        "nk,fkjc->fjnc", sin_inner, imag_grid, precision=precise
    )
    imag_mid = jnp.einsum("nk,fkjc->fjnc", cos_inner, imag_grid, precision=precise) + jnp.einsum(
        "nk,fkjc->fjnc", sin_inner, real_grid, precision=precise
    )
    cos_twist, sin_twist = phase_table(counting(outer_len), counting(inner_len), length)
    cos_twist = cos_twist[None, :, :, None]
    sin_twist = sin_twist[None, :, :, None]
    real_turned = real_mid * cos_twist - imag_mid * sin_twist
    imag_turned = imag_mid * cos_twist + real_mid * sin_twist
    cos_outer, sin_outer = phase_table(counting(outer_len), counting(outer_len), outer_len)
    real_out = jnp.einsum("mj,fjnc->fmnc", cos_outer, real_turned, precision=precise) - jnp.einsum(
        "mj,fjnc->fmnc", sin_outer, imag_turned, precision=precise
    )
    imag_out = jnp.einsum("mj,fjnc->fmnc", cos_outer, imag_turned, precision=precise) + jnp.einsum(
        "mj,fjnc->fmnc", sin_outer, real_turned, precision=precise
    )
    return (real_out.reshape(groups, length, channels), imag_out.reshape(groups, length, channels))


def forward_spectrum(columns, residue_order):
    shards = lax.axis_size("seq")
    local_len = columns.shape[0]
    block_rows = local_len // shards
    freq_rows = 2 * shards
    full_span = freq_rows * local_len
    glob_rows = lax.axis_index("seq") * block_rows + counting(block_rows)
    pieces = lax.all_to_all(columns[None], "seq", split_axis=1, concat_axis=0, tiled=True)
    cos_first, sin_first = phase_table(residue_order, counting(shards), freq_rows)
    real_part = jnp.einsum("ka,amc->kmc", cos_first, pieces[:, :, 0], precision=precise)
    imag_part = -jnp.einsum("ka,amc->kmc", sin_first, pieces[:, :, 0], precision=precise)
    cos_twist, sin_twist = phase_table(residue_order, glob_rows, full_span)
    cos_twist = cos_twist[:, :, None]
    sin_twist = sin_twist[:, :, None]
    real_turned = real_part * cos_twist + imag_part * sin_twist
    imag_turned = imag_part * cos_twist - real_part * sin_twist
    packed = jnp.stack([real_turned, imag_turned], axis=2)
    return local_forward(lax.all_to_all(packed, "seq", split_axis=0, concat_axis=1, tiled=True))


def inverse_signal(real_spec, imag_spec, residue_order):
    shards = lax.axis_size("seq")
    pair_rows = real_spec.shape[0]
    local_len = real_spec.shape[1]
    freq_rows = pair_rows * shards
    full_span = freq_rows * local_len
    real_part, imag_part = local_inverse(real_spec, imag_spec)
    pair_index = lax.dynamic_slice_in_dim(
        residue_order, lax.axis_index("seq") * pair_rows, pair_rows
    )
    cos_twist, sin_twist = phase_table(pair_index, counting(local_len), full_span)
    cos_twist = cos_twist[:, :, None]
    sin_twist = sin_twist[:, :, None]
    real_turned = real_part * cos_twist - imag_part * sin_twist
    imag_turned = imag_part * cos_twist + real_part * sin_twist
    packed = jnp.stack([real_turned, imag_turned], axis=2)
    pieces = lax.all_to_all(packed, "seq", split_axis=1, concat_axis=0, tiled=True)
    cos_last, sin_last = phase_table(counting(shards), residue_order, freq_rows)
    summed = jnp.einsum("ak,kmc->amc", cos_last, pieces[:, :, 0], precision=precise) - jnp.einsum(
        "ak,kmc->amc", sin_last, pieces[:, :, 1], precision=precise
    )
    columns = summed * (1.0 / full_span)
    placed = lax.all_to_all(columns, "seq", split_axis=0, concat_axis=1, tiled=True)
    return placed[0]


def local(sequences, filter_taps, w_in, w_out, grad_out):
    channels = w_out.shape[0]
    groups = lax.axis_size("batch")
    shards = lax.axis_size("seq")
    projected = jnp.dot(sequences[0], w_in, preferred_element_type=jnp.float32)
    queries = projected[:, :channels]
    signal = projected[:, channels : 2 * channels] * projected[:, 2 * channels :]
    back_grad = lax.dot_general(
        grad_out[0], w_out, (((1,), (1,)), ((), ())), preferred_element_type=jnp.float32
    )
    conv_grad = queries * back_grad
    order_table = np.arange(2 * shards)
    residue_order = jnp.asarray(order_table, jnp.int32)
    part_width = channels // groups
    filter_part = lax.dynamic_slice_in_dim(
        filter_taps, lax.axis_index("batch") * part_width, part_width, 1
    )
    signal_spec = forward_spectrum(signal[:, None], residue_order)
    grad_spec = forward_spectrum(conv_grad[:, None], residue_order)
    taps_spec = forward_spectrum(filter_part[:, None], residue_order)
    taps_spec = lax.all_gather(taps_spec, "batch", axis=3, tiled=True)
    real_sig = signal_spec[:, :, 0]
    imag_sig = signal_spec[:, :, 1]
    real_taps = taps_spec[:, :, 0]
    imag_taps = taps_spec[:, :, 1]
    real_conv = real_taps * real_sig - imag_taps * imag_sig
    imag_conv = real_taps * imag_sig + imag_taps * real_sig
    convolved = inverse_signal(real_conv, imag_conv, residue_order)
    gated = (queries * convolved).astype(jnp.bfloat16)
    layer_out = jnp.dot(gated, w_out, preferred_element_type=jnp.float32).astype(jnp.bfloat16)
    factor = 1.0 / (signal_spec.shape[0] * shards * signal_spec.shape[1])
    real_grad = grad_spec[:, :, 0]
    imag_grad = grad_spec[:, :, 1]
    grad_terms = jnp.stack(
        [
            (real_sig * real_grad + imag_sig * imag_grad) * factor,
            (real_sig * imag_grad - imag_sig * real_grad) * factor,
        ],
        axis=0,
    )
    filter_grad = lax.psum_scatter(grad_terms, "batch", scatter_dimension=2, tiled=True)
    return (layer_out[None], filter_grad)


MESH = pl.DeviceIdType.MESH
FULL_TILE = 8


def wide_tables(block_rows, freq_rows):
    residues = freq_rows // 2 + 1
    span = block_rows * freq_rows
    near = np.arange(block_rows)
    angles = 2.0 * np.pi * (np.outer(near, near) % block_rows) / block_rows
    cos_part, sin_part = np.cos(angles), np.sin(angles)
    matrix = np.block([[cos_part, -sin_part], [sin_part, cos_part]])
    high = matrix.astype(jnp.bfloat16)
    low = (matrix - high.astype(np.float64)).astype(jnp.bfloat16)
    twist_angles = 2.0 * np.pi * np.outer(np.arange(residues), near) / span
    twist = np.stack([np.cos(twist_angles), np.sin(twist_angles)], axis=0).astype(np.float32)
    twist = np.ascontiguousarray(
        np.broadcast_to(twist[:, :, None, :], (2, residues, FULL_TILE, block_rows))
    )
    return (high, low, twist)


def grouped_sum(items, weights):
    groups = {}
    for item, weight in zip(items, weights):
        size = round(abs(weight), 12)
        if size == 0.0:
            continue
        positive, total = groups.get(size, (None, None))
        if total is None:
            groups[size] = (weight > 0, item)
        elif positive == (weight > 0):
            groups[size] = (positive, total + item)
        else:
            groups[size] = (positive, total - item)
    result = None
    for size in sorted(groups, reverse=True):
        positive, total = groups[size]
        term = total if size == 1.0 else total * size
        if result is None:
            result = term if positive else -term
        else:
            result = result + term if positive else result - term
    return result


def kernel(
    groups, shards, part,
    x_hbm, taps_hbm, w_in_hbm, w_out_hbm, cot_hbm, high_hbm, low_hbm, twist_hbm,
    out_ref, spec_out,
    x_ref, taps_ref, w_in_ref, w_out_ref, cot_ref, high_ref, low_ref, twist_ref,
    load_sems, query_buf, sig_send, cot_send, tap_send, sig_buf, cot_buf, tap_buf,
    conv_send, conv_buf, spec_send, near_sig, near_tap, near_conv,
    work, sig_spec, tap_spec, near_sig_spec, near_tap_spec, send_sems, recv_sems, late,
):
    count = groups * shards
    rows = x_ref.shape[1]
    channels = w_out_ref.shape[0]
    half = shards // 2
    quarter = shards // 4
    lanes = rows // groups
    my_group = lax.axis_index("batch")
    my_shard = lax.axis_index("seq")
    me = my_group * shards + my_shard
    my_half = lax.div(my_shard, half)
    lower = my_half == 0
    upper = my_half == 1
    is_last = my_shard >= shards - quarter
    near_me = my_group * half + lax.rem(my_shard, half)
    barrier = pltpu.get_barrier_semaphore()

    def across(step):
        turn = step // groups
        shard = (1 - my_half) * half + turn // quarter * quarter + lax.rem(my_shard + turn, quarter)
        return (lax.rem(my_group + step, groups), shard)

    def level(step):
        turn = step // groups
        shard = lax.div(my_shard, quarter) * quarter + lax.rem(my_shard + turn, quarter)
        return (lax.rem(my_group + step, groups), shard)

    def beside(step):
        turn = step // groups
        plane = 2 * my_half + 1 - lax.rem(lax.div(my_shard, quarter), 2)
        return (lax.rem(my_group + step, groups), plane * quarter + lax.rem(my_shard + turn, quarter))

    wide = groups * quarter
    far_first = [across(step) for step in range(wide)]
    far_second = [across(step) for step in range(wide, 2 * wide)]
    far = far_first + far_second
    same_plane = [level(step) for step in range(1, wide)]
    next_plane = [beside(step) for step in range(wide)]
    near = next_plane + same_plane

    def signal(semaphore, peers):
        for group, shard in peers:
            pl.semaphore_signal(semaphore, inc=1, device_id=(group, shard), device_id_type=MESH)

    @pl.when(jnp.logical_not(is_last))
    def _():
        signal(barrier, far + near)

    @pl.when(is_last)
    def _():
        signal(barrier, same_plane)

    loads = [
        pltpu.make_async_copy(source, target, load_sems.at[n])
        for n, (source, target) in enumerate(
            (
                (x_hbm, x_ref),
                (w_in_hbm, w_in_ref),
                (taps_hbm, taps_ref),
                (w_out_hbm, w_out_ref),
                (cot_hbm, cot_ref),
                (twist_hbm, twist_ref),
                (high_hbm, high_ref),
                (low_hbm, low_ref),
            )
        )
    ]
    for load in loads:
        load.start()

    def push(source, target, slot, peers):
        for group, shard in peers:
            pltpu.make_async_remote_copy(
                src_ref=source.at[group * shards + shard],
                dst_ref=target.at[me],
                send_sem=send_sems.at[slot],
                recv_sem=recv_sems.at[slot],
                device_id=(group, shard),
                device_id_type=MESH,
            ).start()

    def push_taps(turns, opposite):
        base = (my_half + opposite - 2 * my_half * opposite) * half
        for turn in turns:
            shard = base + lax.rem(my_shard + turn, half)
            pltpu.make_async_remote_copy(
                src_ref=tap_send.at[my_group * shards + shard],
                dst_ref=tap_buf.at[my_shard],
                send_sem=send_sems.at[1],
                recv_sem=recv_sems.at[1],
                device_id=(my_group, shard),
                device_id_type=MESH,
            ).start()

    def bundle(source, target, slot, many):
        return pltpu.make_async_remote_copy(
            src_ref=source.at[pl.ds(0, many)],
            dst_ref=target.at[pl.ds(0, many)],
            send_sem=send_sems.at[slot],
            recv_sem=recv_sems.at[slot],
            device_id=(my_group, my_shard),
            device_id_type=MESH,
        )

    loads[0].wait()
    loads[1].wait()
    projected = lax.dot_general(
        w_in_ref[...], x_ref[0], (((0,), (1,)), ((), ())), preferred_element_type=jnp.float32
    )
    queries = projected[:channels]
    query_buf[...] = queries
    signal_part = projected[channels : 2 * channels] * projected[2 * channels :]
    sig_send[...] = signal_part.reshape(count, part, rows)
    loads[2].wait()
    tap_send[...] = taps_ref[...].T.reshape(count, part, rows)
    pl.semaphore_wait(barrier, jnp.where(is_last, count - 1, count - 1 - wide))

    @pl.when(is_last)
    def _():
        signal(late, far + next_plane)

    @pl.when(lower)
    def _():
        push(sig_send, sig_buf, 0, far_first + near)
        for group, shard in near:
            pltpu.make_async_remote_copy(
                src_ref=sig_send.at[group * shards + shard + half],
                dst_ref=near_sig.at[near_me],
                send_sem=send_sems.at[5],
                recv_sem=recv_sems.at[5],
                device_id=(group, shard),
                device_id_type=MESH,
            ).start()
        near_sig[near_me] = sig_send[me + half]
        for offset in range(1, half):
            shard = lax.rem(my_shard + offset, half)
            pltpu.make_async_remote_copy(
                src_ref=tap_send.at[my_group * shards + shard + half],
                dst_ref=near_tap.at[my_shard],
                send_sem=send_sems.at[6],
                recv_sem=recv_sems.at[6],
                device_id=(my_group, shard),
                device_id_type=MESH,
            ).start()
        near_tap[my_shard] = tap_send[me + half]

    @pl.when(upper)
    def _():
        push(sig_send, sig_buf, 0, far)
        push_taps(range(half), 1)
        push(sig_send, sig_buf, 0, same_plane)

    sig_buf[me] = sig_send[me]
    tap_buf[my_shard] = tap_send[me]
    loads[3].wait()
    loads[4].wait()
    back = lax.dot_general(
        w_out_ref[...], cot_ref[0], (((1,), (1,)), ((), ())), preferred_element_type=jnp.float32
    )
    cot_send[...] = (queries * back).reshape(count, part, rows)

    @pl.when(jnp.logical_not(is_last))
    def _():
        pl.semaphore_wait(late, wide)

    @pl.when(lower)
    def _():
        push(sig_send, sig_buf, 0, far_second)

    @pl.when(upper)
    def _():
        push(sig_send, sig_buf, 0, next_plane)

    @pl.when(lower)
    def _():
        push_taps(range(1, half), 0)

    push(cot_send, cot_buf, 2, far)

    @pl.when(lower)
    def _():
        push_taps(range(half), 1)

    push(cot_send, cot_buf, 2, near)

    @pl.when(upper)
    def _():
        push_taps(range(1, half), 0)

    cot_buf[me] = cot_send[me]

    def multiply(value):
        top = value.astype(jnp.bfloat16)
        rest = (value - top.astype(jnp.float32)).astype(jnp.bfloat16)
        high = high_ref[...]
        return (
            jnp.dot(top, high, preferred_element_type=jnp.float32)
            + jnp.dot(rest, high, preferred_element_type=jnp.float32)
            + jnp.dot(top, low_ref[...], preferred_element_type=jnp.float32)
        )

    for load in loads[5:]:
        load.wait()

    def forward(blocks, height):
        bands = len(blocks)
        turns = math.pi / bands
        for index in range(bands + 1):
            real_part = grouped_sum(
                blocks, [math.cos(turns * (a * index % (2 * bands))) for a in range(bands)]
            )
            imag_part = grouped_sum(
                blocks, [-math.sin(turns * (a * index % (2 * bands))) for a in range(bands)]
            )
            cos_t = twist_ref[0, index * (shards // bands)][None]
            sin_t = twist_ref[1, index * (shards // bands)][None]
            if imag_part is None:
                real_turned = real_part * cos_t
                imag_turned = -(real_part * sin_t)
            else:
                real_turned = real_part * cos_t + imag_part * sin_t
                imag_turned = imag_part * cos_t - real_part * sin_t
            place_at = pl.ds(index * height, height)
            work[place_at, :rows] = real_turned.reshape(height, rows)
            work[place_at, rows:] = imag_turned.reshape(height, rows)
        return multiply(work[pl.ds(0, (bands + 1) * height), :])

    height = groups * part

    def convolve(bands, sig_from, tap_from, target):
        turns = math.pi / bands
        scale = 1.0 / (2 * bands * rows)
        used = pl.ds(0, (bands + 1) * height)
        for index in range(bands + 1):
            weight = scale if index in (0, bands) else 2.0 * scale
            tap_part = tap_from[pl.ds(index * part, part), :] * weight
            real_tap = tap_part[None, :, :rows]
            imag_tap = tap_part[None, :, rows:]
            sig_part = sig_from[pl.ds(index * height, height), :].reshape(groups, part, 2 * rows)
            real_sig = sig_part[:, :, :rows]
            imag_sig = sig_part[:, :, rows:]
            place_at = pl.ds(index * height, height)
            work[place_at, :rows] = (real_tap * real_sig - imag_tap * imag_sig).reshape(height, rows)
            work[place_at, rows:] = -(real_tap * imag_sig + imag_tap * real_sig).reshape(height, rows)
        work[used, :] = multiply(work[used, :])
        real_items = []
        imag_items = []
        for index in range(bands + 1):
            piece = work[pl.ds(index * height, height), :].reshape(groups, part, 2 * rows)
            cos_t = twist_ref[0, index * (shards // bands)][None]
            sin_t = twist_ref[1, index * (shards // bands)][None]
            real_items.append(piece[:, :, :rows] * cos_t + piece[:, :, rows:] * sin_t)
            imag_items.append(piece[:, :, :rows] * sin_t - piece[:, :, rows:] * cos_t)
        for a in range(bands):
            value = grouped_sum(
                real_items + imag_items,
                [math.cos(turns * (a * i % (2 * bands))) for i in range(bands + 1)]
                + [-math.sin(turns * (a * i % (2 * bands))) for i in range(bands + 1)],
            )
            for group in range(groups):
                target[group * bands + a] = value[group]

    bundle(sig_send, sig_buf, 0, count - 1).wait_recv()
    by_source = sig_buf[...].reshape(groups, shards, part, rows)
    sig_spec[...] = forward([by_source[:, a] for a in range(shards)], height)

    def respond():
        bundle(tap_send, tap_buf, 1, shards - 1).wait_recv()
        tap_blocks = tap_buf[...]
        tap_spec[...] = forward([tap_blocks[a][None] for a in range(shards)], part)
        convolve(shards, sig_spec, tap_spec, conv_send)

    @pl.when(lower)
    def _():
        respond()
        push(conv_send, conv_buf, 3, far + near)
        conv_buf[me] = conv_send[me]

    @pl.when(lower)
    def _():
        bundle(sig_send, near_sig, 5, groups * half - 1).wait_recv()
        by_source = near_sig[...].reshape(groups, half, part, rows)
        near_sig_spec[...] = forward(
            [by_source[:, a] for a in range(half)], height
        )
        bundle(tap_send, near_tap, 6, half - 1).wait_recv()
        tap_blocks = near_tap[...]
        near_tap_spec[...] = forward(
            [tap_blocks[a][None] for a in range(half)], part
        )
        convolve(half, near_sig_spec, near_tap_spec, near_conv)
        for group, shard in near:
            pltpu.make_async_remote_copy(
                src_ref=near_conv.at[group * half + shard],
                dst_ref=conv_buf.at[me + half],
                send_sem=send_sems.at[7],
                recv_sem=recv_sems.at[3],
                device_id=(group, shard),
                device_id_type=MESH,
            ).start()
        conv_buf[me + half] = near_conv[near_me]

    factor = 1.0 / (2 * shards * rows)
    residues = shards + 1
    bundle(cot_send, cot_buf, 2, count - 1).wait_recv()
    by_source = cot_buf[...].reshape(groups, shards, part, rows)
    work[...] = forward([by_source[:, a] for a in range(shards)], height)
    real_spec = []
    imag_spec = []
    for index in range(residues):
        place_at = pl.ds(index * height, height)
        sig_part = (sig_spec[place_at, :] * factor).reshape(groups, part, 2 * rows)
        cot_part = work[place_at, :].reshape(groups, part, 2 * rows)
        real_sig, imag_sig = sig_part[:, :, :rows], sig_part[:, :, rows:]
        real_cot, imag_cot = cot_part[:, :, :rows], cot_part[:, :, rows:]
        real_spec.append(jnp.sum(real_sig * real_cot + imag_sig * imag_cot, axis=0))
        imag_spec.append(jnp.sum(real_sig * imag_cot - imag_sig * real_cot, axis=0))
    row = lax.broadcasted_iota(jnp.int32, (rows, rows), 0)
    column = lax.broadcasted_iota(jnp.int32, (rows, rows), 1)
    reverse = jnp.where(row + column == rows - 1, 1.0, 0.0).astype(jnp.bfloat16)
    straight = jnp.concatenate(
        real_spec[1:shards] + [-piece for piece in imag_spec[1:shards]], axis=0
    )
    turned = None
    for _ in range(3):
        top = straight.astype(jnp.bfloat16)
        straight = straight - top.astype(jnp.float32)
        term = jnp.dot(top, reverse, preferred_element_type=jnp.float32)
        turned = term if turned is None else turned + term
    for index in range(shards - 1, 0, -1):
        low_row = (index - 1) * part
        real_spec.append(turned[low_row : low_row + part])
        low_row += (shards - 1) * part
        imag_spec.append(turned[low_row : low_row + part])
    for shard in range(shards):
        for group in range(groups):
            pieces = [
                spec[index][:, group * lanes : (group + 1) * lanes]
                for spec in (real_spec, imag_spec)
                for index in (2 * shard, 2 * shard + 1)
            ]
            spec_send[group * shards + shard] = jnp.concatenate(pieces, axis=1)

    def line(turn):
        shard = ((1 - my_half) * 2 + turn // quarter) * quarter + turn % quarter
        return [(lax.rem(my_group + c, groups), shard) for c in range(groups)]

    @pl.when(lower)
    def _():
        turns = [quarter, *range(quarter), *range(quarter + 1, 2 * quarter)]
        push(spec_send, spec_out, 4, [peer for turn in turns for peer in line(turn)] + near)

    @pl.when(upper)
    def _():
        push(spec_send, spec_out, 4, far + near)

    @pl.when(upper)
    def _():
        respond()
        push(conv_send, conv_buf, 3, near)
        conv_buf[me] = conv_send[me]

    spec_out[me] = spec_send[me]

    @pl.when(lower)
    def _():
        bundle(conv_send, conv_buf, 3, count - 2).wait_recv()

    @pl.when(upper)
    def _():
        bundle(conv_send, conv_buf, 3, count - 1).wait_recv()

    gated = (query_buf[...] * conv_buf[...].reshape(channels, rows)).astype(jnp.bfloat16)
    out_ref[0] = lax.dot_general(
        gated, w_out_ref[...], (((0,), (0,)), ((), ())), preferred_element_type=jnp.float32
    ).astype(jnp.bfloat16)

    bundle(sig_send, sig_buf, 0, count - 1).wait_send()
    bundle(tap_send, tap_buf, 1, shards - 1).wait_send()
    bundle(cot_send, cot_buf, 2, count - 1).wait_send()

    @pl.when(lower)
    def _():
        bundle(conv_send, conv_buf, 3, count - 1).wait_send()
        bundle(sig_send, near_sig, 5, groups * half - 1).wait_send()
        bundle(tap_send, near_tap, 6, half - 1).wait_send()
        bundle(near_conv, conv_buf, 7, groups * half - 1).wait_send()

    @pl.when(upper)
    def _():
        bundle(conv_send, conv_buf, 3, groups * half - 1).wait_send()

    bundle(spec_send, spec_out, 4, count - 1).wait_send()
    bundle(spec_send, spec_out, 4, count - 1).wait_recv()


def finish(raw_buf, spec_buf, out_hbm, grad_hbm, grad_buf, store_sems):
    stores = [pltpu.make_async_copy(raw_buf, out_hbm, store_sems.at[2])]
    stores[0].start()
    count, part, width = spec_buf.shape
    for kind in range(2):
        piece = spec_buf[:, :, kind * (width // 2) : (kind + 1) * (width // 2)]
        grad_buf[kind] = piece.reshape(count * part, width // 2).T.reshape(grad_buf.shape[1:])
        store = pltpu.make_async_copy(grad_buf.at[kind], grad_hbm.at[kind], store_sems.at[kind])
        store.start()
        stores.append(store)
    for store in stores:
        store.wait()


def direct(sequences, filter_taps, w_in, w_out, grad_out):
    groups = lax.axis_size("batch")
    shards = lax.axis_size("seq")
    rows = sequences.shape[1]
    channels = w_out.shape[0]
    count = groups * shards
    part = channels // count
    freq_rows = 2 * shards
    residues = shards + 1
    lanes = rows // groups
    high, low, twist = wide_tables(rows, freq_rows)
    operands = (
        sequences, filter_taps, w_in, w_out, grad_out,
        jnp.asarray(high), jnp.asarray(low), jnp.asarray(twist),
    )
    chunk = pltpu.VMEM((count, part, rows), jnp.float32)
    height = groups * part
    anywhere = pl.BlockSpec(memory_space=pl.ANY)
    on_chip = pl.BlockSpec(memory_space=pltpu.VMEM)
    raw, spectra = pl.pallas_call(
        functools.partial(kernel, groups, shards, part),
        out_shape=(
            pltpu.VMEM((1, rows, channels), jnp.bfloat16),
            pltpu.VMEM((count, part, rows), jnp.float32),
        ),
        in_specs=[anywhere] * 8,
        out_specs=(on_chip, on_chip),
        scratch_shapes=[
            *(pltpu.VMEM(item.shape, item.dtype) for item in operands),
            pltpu.SemaphoreType.DMA((8,)),
            pltpu.VMEM((channels, rows), jnp.float32),
            chunk,
            chunk,
            chunk,
            chunk,
            chunk,
            pltpu.VMEM((shards, part, rows), jnp.float32),
            chunk,
            chunk,
            chunk,
            pltpu.VMEM((count // 2, part, rows), jnp.float32),
            pltpu.VMEM((shards // 2, part, rows), jnp.float32),
            pltpu.VMEM((count // 2, part, rows), jnp.float32),
            pltpu.VMEM((residues * height, 2 * rows), jnp.float32),
            pltpu.VMEM((residues * height, 2 * rows), jnp.float32),
            pltpu.VMEM((residues * part, 2 * rows), jnp.float32),
            pltpu.VMEM(((shards // 2 + 1) * height, 2 * rows), jnp.float32),
            pltpu.VMEM(((shards // 2 + 1) * part, 2 * rows), jnp.float32),
            pltpu.SemaphoreType.DMA((8,)),
            pltpu.SemaphoreType.DMA((7,)),
            pltpu.SemaphoreType.REGULAR,
        ],
        compiler_params=pltpu.CompilerParams(collective_id=0, has_side_effects=True),
    )(*operands)
    return pl.pallas_call(
        finish,
        out_shape=(
            jax.ShapeDtypeStruct((1, rows, channels), jnp.bfloat16),
            jax.ShapeDtypeStruct((2, 2, lanes, channels), jnp.float32),
        ),
        in_specs=[on_chip] * 2,
        out_specs=(anywhere, anywhere),
        scratch_shapes=[
            pltpu.VMEM((2, 2, lanes, channels), jnp.float32),
            pltpu.SemaphoreType.DMA((3,)),
        ],
    )(
        pltpu.with_memory_space_constraint(raw, pltpu.VMEM),
        pltpu.with_memory_space_constraint(spectra, pltpu.VMEM),
    )


def body(sequences, filter_taps, w_in, w_out, grad_out):
    groups = lax.axis_size("batch")
    count = groups * lax.axis_size("seq")
    rows = sequences.shape[1]
    fits = (
        sequences.shape[0] == 1
        and w_out.shape[0] == FULL_TILE * count
        and lax.axis_size("seq") % 4 == 0
        and rows % 128 == 0
        and rows % groups == 0
        and 2 * (rows // groups) % 128 == 0
    )
    chosen = direct if fits else local
    return chosen(sequences, filter_taps, w_in, w_out, grad_out)


def solution(mesh):
    placed = (P("batch", "seq", None), P("seq", None), P(), P(), P("batch", "seq", None))
    return jax.shard_map(
        body,
        mesh=mesh,
        in_specs=placed,
        out_specs=(P("batch", "seq", None), P(None, "seq", "batch", None)),
        check_vma=False,
    )
```
